32 devices in a mesh: dp: 16 (over z, y, x), tensor: 2 (over core).
Axes of the slice: x: 2, y: 2, z: 4, core: 2. Of those that a mesh axis runs over, the one named last changes fastest.
Arguments:
- tokens: bfloat16 [25088, 768], P('dp'), may hold values from -6 to 6
- cotangent: bfloat16 [25088, 768], P('dp'), may hold values from -18 to 18
- w_qkv: bfloat16 [768, 3, 768], P(None, None, 'tensor'), may hold values from -0.21875 to 0.21875
- qv_bias: bfloat16 [2, 768], P(None, 'tensor'), may hold values from -3 to 3
- w_proj: bfloat16 [768, 768], P('tensor'), may hold values from -0.875 to 0.875
- proj_bias: bfloat16 [768], replicated, may hold values from -2 to 2
- w_fc1: bfloat16 [768, 3072], P(None, 'tensor'), may hold values from -0.21875 to 0.21875
- fc1_bias: bfloat16 [3072], P('tensor'), may hold values from -3 to 3
- w_fc2: bfloat16 [3072, 768], P('tensor'), may hold values from -0.109375 to 0.109375
- fc2_bias: bfloat16 [768], replicated, may hold values from -2 to 2
- gain_one: bfloat16 [768], replicated, may hold values from 0.5 to 1.5
- shift_one: bfloat16 [768], replicated, may hold values from -2 to 2
- gain_two: bfloat16 [768], replicated, may hold values from 0.5 to 1.5
- shift_two: bfloat16 [768], replicated, may hold values from -2 to 2
- rel_h: bfloat16 [27, 64], replicated, may hold values from -1 to 1
- rel_w: bfloat16 [27, 64], replicated, may hold values from -1 to 1
Outputs:
- output: bfloat16 [25088, 768], P('dp')
- d_tokens: bfloat16 [25088, 768], P('dp')
- d_w_qkv: float32 [768, 3, 768], P(None, None, 'tensor')
- d_qv_bias: float32 [2, 768], P(None, 'tensor')
- d_w_proj: float32 [768, 768], P('tensor')
- d_proj_bias: float32 [768], replicated
- d_w_fc1: float32 [768, 3072], P(None, 'tensor')
- d_fc1_bias: float32 [3072], P('tensor')
- d_w_fc2: float32 [3072, 768], P('tensor')
- d_fc2_bias: float32 [768], replicated
- d_gain_one: float32 [768], replicated
- d_shift_one: float32 [768], replicated
- d_gain_two: float32 [768], replicated
- d_shift_two: float32 [768], replicated
- d_rel_h: float32 [27, 64], replicated
- d_rel_w: float32 [27, 64], replicated
The draws below stay inside these ranges and needn't reach their ends.
All inputs are finite; a program needn't handle non-finite values.
Results may differ from the reference program's by a relative error of at most 0.012.
The reference program's roundings to bfloat16 on the way count: a program that leaves them out, or rounds other values in their place, can miss the bound.
Values sent between devices are 32-bit elements; how exact they have to be, the bound alone decides.
No kernel may reach another device: no remote copies, remote signals or barrier semaphores. Data moves between devices by JAX's collectives and lax.ppermute only.
A program may use at most 256 MiB of HBM per device.

```python
import jax
import jax.numpy as jnp
from jax import lax

D = 768
HEADS = 12
HEAD_DIM = 64
FF = 3072
WIN = 14
IMG = 64
WIN_DEV = 8
GRID = 5
RELS = 27
WINDOWS = 128
ROWS = 25088


def draw_cotangent(key, part):
    row_total = WINDOWS * WIN * WIN
    noise_draw = jnp.clip(jax.random.normal(key, (row_total, D), jnp.float32), -6.0, 6.0)
    window_pos = (jnp.arange(row_total, dtype=jnp.int32) // (WIN * WIN)).astype(jnp.float32)
    ramp_scale = 1.0 + 2.0 * window_pos / max(WINDOWS - 1, 1)
    return (noise_draw * ramp_scale[:, None]).astype(jnp.bfloat16)


def shard_levels(stream_key, shape, shards, low, top_value):
    def one(dim, blocks):
        heights = jax.random.uniform(jax.random.fold_in(jax.random.fold_in(stream_key, 6), dim), (blocks,), jnp.float32, low / len(shards), top_value / len(shards))
        return jnp.repeat(jnp.exp(heights), shape[dim] // blocks).reshape((-1,) + (1,) * (len(shape) - dim - 1))

    gain = one(*shards[0])
    for cut in shards[1:]:
        gain = gain * one(*cut)
    return gain


def normal_values(stream_key, dims, deviation, limit, cuts=(), kind=jnp.bfloat16):
    drawn = deviation * jax.random.normal(stream_key, dims, jnp.float32)
    if cuts:
        drawn = drawn * shard_levels(stream_key, dims, cuts, -0.22, 0.18)
    return jnp.clip(drawn, -limit, limit).astype(kind)


def setup_inputs(seed: int = 0) -> dict:
    seeds = jax.random.split(jax.random.key(seed), 17)
    return {
        "tokens": normal_values(seeds[0], (ROWS, D), 1.0, 6.0, ((0, 16),)),
        "cotangent": draw_cotangent(jax.random.fold_in(seeds[16], 71), 0),
        "w_qkv": normal_values(seeds[2], (D, 3, D), D ** -0.5, 0.21875, ((2, 2),)),
        "qv_bias": normal_values(seeds[3], (2, D), 0.5, 3.0, ((1, 2),)),
        "w_proj": normal_values(seeds[4], (D, D), (D // 16) ** -0.5, 0.875, ((0, 2),)),
        "proj_bias": normal_values(seeds[5], (D,), 0.3, 2.0),
        "w_fc1": normal_values(seeds[6], (D, FF), D ** -0.5, 0.21875, ((1, 2),)),
        "fc1_bias": normal_values(seeds[7], (FF,), 0.5, 3.0, ((0, 2),)),
        "w_fc2": normal_values(seeds[8], (FF, D), FF ** -0.5, 0.109375, ((0, 2),)),
        "fc2_bias": normal_values(seeds[9], (D,), 0.3, 2.0),
        "gain_one": jnp.clip(1.0 + 0.1 * jax.random.normal(seeds[10], (D,), jnp.float32), 0.5, 1.5).astype(jnp.bfloat16),
        "shift_one": normal_values(seeds[11], (D,), 0.3, 2.0),
        "gain_two": jnp.clip(1.0 + 0.1 * jax.random.normal(seeds[12], (D,), jnp.float32), 0.5, 1.5).astype(jnp.bfloat16),
        "shift_two": normal_values(seeds[13], (D,), 0.3, 2.0),
        "rel_h": normal_values(seeds[14], (RELS, HEAD_DIM), 0.15, 1.0),
        "rel_w": normal_values(seeds[15], (RELS, HEAD_DIM), 0.15, 1.0),
    }


@jax.custom_vjp
def low(v):
    return lax.optimization_barrier(v.astype(jnp.bfloat16)).astype(jnp.float32)

@jax.custom_vjp
def low_back(v):
    return v

def low_keep(v):
    return (low(v), None)

def low_pass(kept, grad):
    return (grad,)

def back_keep(v):
    return (v, None)

def back_low(kept, grad):
    return (low(grad),)
low.defvjp(low_keep, low_pass)
low_back.defvjp(back_keep, back_low)
NORM_EPS = 1e-06
PRECISE = lax.Precision.HIGHEST

def layer_norm(inputs, norm_gain, norm_shift):
    mean_val = lax.optimization_barrier(jnp.mean(inputs, axis=-1, keepdims=True))
    centered = inputs - mean_val
    variance = lax.optimization_barrier(jnp.mean(centered * centered, axis=-1, keepdims=True))
    return centered * lax.rsqrt(variance + NORM_EPS) * norm_gain + norm_shift

def gelu_exact(inputs):
    return 0.5 * inputs * (1.0 + jax.scipy.special.erf(inputs * 0.7071067811865476))

def row_mask(row_count):
    row_index = jnp.arange(row_count, dtype=jnp.int32)
    window = row_index // (WIN * WIN)
    inner_pos = row_index % (WIN * WIN)
    grid_cell = window % (GRID * GRID)
    row_pos = grid_cell // GRID * WIN + inner_pos // WIN
    col_pos = grid_cell % GRID * WIN + inner_pos % WIN
    return ((row_pos < IMG) & (col_pos < IMG)).astype(jnp.float32)[:, None]

def offsets():
    near_index = jnp.arange(WIN, dtype=jnp.int32)
    return near_index[:, None] - near_index[None, :] + WIN - 1

def group_forward(params, group_rows, group_mask):
    w_qkv, qv_bias, w_proj, proj_bias, w_fc1, fc1_bias, w_fc2, fc2_bias, gain_one, shift_one, gain_two, shift_two, rel_h, rel_w = params
    row_count = group_rows.shape[0]
    win_count = row_count // (WIN * WIN)
    hidden_one = low(group_mask * layer_norm(group_rows, gain_one, shift_one))
    qkv = jnp.dot(hidden_one, w_qkv.reshape(D, 3 * D), precision=PRECISE).reshape(row_count, 3, D)
    queries = low(low_back(qkv[:, 0] + qv_bias[0]))
    keys_low = low(low_back(qkv[:, 1]))
    values_low = low(low_back(qkv[:, 2] + qv_bias[1]))
    q_six = queries.reshape(win_count, WIN, WIN, HEADS, HEAD_DIM)
    k_four = keys_low.reshape(win_count, WIN * WIN, HEADS, HEAD_DIM)
    v_four = values_low.reshape(win_count, WIN * WIN, HEADS, HEAD_DIM)
    table_h = rel_h[offsets()]
    table_w = rel_w[offsets()]
    base = jnp.einsum('bqhc,bkhc->bhqk', q_six.reshape(win_count, WIN * WIN, HEADS, HEAD_DIM), k_four, precision=PRECISE) * HEAD_DIM ** (-0.5)
    near_h = jnp.einsum('bijhc,ikc->bhijk', q_six, table_h, precision=PRECISE)
    near_w = jnp.einsum('bijhc,jlc->bhijl', q_six, table_w, precision=PRECISE)
    scores = base.reshape(win_count, HEADS, WIN, WIN, WIN, WIN) + near_h[..., :, None] + near_w[..., None, :]
    scores = low_back(scores.reshape(win_count, HEADS, WIN * WIN, WIN * WIN))
    row_max = lax.optimization_barrier(jnp.max(scores, axis=-1, keepdims=True))
    exp_terms = jnp.exp(scores - row_max)
    attn_probs = low(exp_terms / lax.optimization_barrier(jnp.sum(exp_terms, axis=-1, keepdims=True)))
    context = jnp.einsum('bhqk,bkhc->bqhc', attn_probs, v_four, precision=PRECISE).reshape(row_count, D)
    context = low(low_back(context))
    attention = low_back(jnp.dot(context, w_proj, precision=PRECISE)) + proj_bias
    y_one = group_rows + attention
    hidden_two = low(layer_norm(y_one, gain_two, shift_two))
    pre_act = low_back(jnp.dot(hidden_two, w_fc1, precision=PRECISE) + fc1_bias)
    activation = low(gelu_exact(pre_act))
    mlp_out = low_back(jnp.dot(activation, w_fc2, precision=PRECISE)) + fc2_bias
    return group_mask * (y_one + mlp_out)

def reference(tokens, cotangent, w_qkv, qv_bias, w_proj, proj_bias, w_fc1, fc1_bias, w_fc2, fc2_bias, gain_one, shift_one, gain_two, shift_two, rel_h, rel_w):
    params = tuple((item.astype(jnp.float32) for item in (w_qkv, qv_bias, w_proj, proj_bias, w_fc1, fc1_bias, w_fc2, fc2_bias, gain_one, shift_one, gain_two, shift_two, rel_h, rel_w)))
    tok_wide = tokens.astype(jnp.float32)
    row_total = tokens.shape[0]
    group_count = row_total // (WIN_DEV * WIN * WIN)
    all_mask = row_mask(row_total)

    def forward(param_set, inputs):
        grouped = inputs.reshape(group_count, -1, D)
        masks_grouped = all_mask.reshape(group_count, -1, 1)
        group_step = jax.checkpoint(lambda rows_in, mask_in: group_forward(param_set, rows_in, mask_in))

        def scan_body(state_carry, inputs_pair):
            return (state_carry, group_step(inputs_pair[0], inputs_pair[1]))
        _, results = lax.scan(scan_body, None, (grouped, masks_grouped))
        return results.reshape(row_total, D)
    output, pull_back = jax.vjp(forward, params, tok_wide)
    weight_grads, d_tokens = pull_back(cotangent.astype(jnp.float32))
    return (output.astype(jnp.bfloat16), d_tokens.astype(jnp.bfloat16), weight_grads[0], weight_grads[1], weight_grads[2], weight_grads[3], weight_grads[4], weight_grads[5], weight_grads[6], weight_grads[7], weight_grads[8], weight_grads[9], weight_grads[10], weight_grads[11], weight_grads[12], weight_grads[13])
```

```python
import functools
import jax
import jax.numpy as jnp
from jax import lax
from jax.experimental import pallas as pl
from jax.experimental.pallas import tpu as pltpu
from jax.sharding import PartitionSpec as P

IMG = 64
GRID = 5

HEAD_DIM = 64
WIN = 14
TOK = WIN * WIN
PADW = 208
NEG = -1e30
EPS = 1e-6
SCALE = HEAD_DIM ** -0.5
NT = (((1,), (1,)), ((), ()))
TN = (((0,), (0,)), ((), ()))
NN = (((1,), (0,)), ((), ()))


def mm(a, b, dims=NN):
    return lax.dot_general(a, b, dims, preferred_element_type=jnp.float32)


def rel_matrix(rel_h, rel_w):
    pad = jnp.zeros((5, HEAD_DIM), rel_h.dtype)
    near = jnp.concatenate([rel_h[::-1], pad, rel_w[::-1], pad], 0)
    zero = jnp.zeros_like(near)
    return jnp.concatenate(
        [jnp.concatenate([zero, near.T], 1), jnp.concatenate([near.T, zero], 1)], 0
    )


def key_matrix():
    key = jnp.arange(PADW)[:, None]
    lane = jnp.arange(128)[None, :] % 64
    real = key < TOK
    slot = lane % 16
    hot = jnp.where(lane < 32, key // WIN == slot, key % WIN == slot) & real & (slot < WIN)
    once = hot & (lane % 32 < 16)
    neg = jnp.where((lane == 30) & ~real, NEG, 0.0)
    return (hot.astype(jnp.float32) + neg).astype(jnp.bfloat16), once.astype(jnp.bfloat16)


def shift_table():
    row = jnp.minimum(jnp.arange(PADW), TOK - 1)[:, None]
    lane = jnp.arange(128)[None, :] % 64
    return jnp.where(lane < 32, WIN - 1 - row // WIN, WIN - 1 - row % WIN).astype(jnp.int32)


def lanes():
    return lax.broadcasted_iota(jnp.int32, (PADW, 128), 1)


def fwd_kernel(x_ref, keep_ref, gain_ref, shift_ref, w_ref, bias_ref, rel_ref, hot_ref, tab_ref,
               hid_ref, qkv_ref, prob_ref, ctx_ref, acc_ref):
    x = x_ref[...].astype(jnp.float32)
    mean = jnp.mean(x, axis=1, keepdims=True)
    cen = x - mean
    var = jnp.mean(cen * cen, axis=1, keepdims=True)
    h = cen * lax.rsqrt(var + EPS) * gain_ref[...] + shift_ref[...]
    h = (h * keep_ref[...]).astype(jnp.bfloat16)
    hid_ref[...] = h
    width = w_ref.shape[2]
    for t in range(3):
        acc_ref[:, t * width:(t + 1) * width] = mm(h, w_ref[t]) + bias_ref[t:t + 1]
    lane = lanes()
    low_half = lane < 64
    slot = lane % 32
    near_ok = slot < WIN
    one_lane = lane % 64 == 30
    tab = tab_ref[...]
    bits = [(tab & (1 << b)) != 0 for b in range(4)]
    hot = hot_ref[...]
    for w in range(x_ref.shape[0] // TOK):
        rows = acc_ref[w * TOK:(w + 1) * TOK, :]
        qkv_ref[w, :TOK, :] = rows.astype(jnp.bfloat16)
        qkv_ref[w, TOK:, :] = jnp.zeros((PADW - TOK, 3 * width), jnp.bfloat16)
        for p in range(width // 128):
            q = qkv_ref[w, :, p * 128:(p + 1) * 128]
            k = qkv_ref[w, :, width + p * 128:width + (p + 1) * 128]
            v = qkv_ref[w, :, 2 * width + p * 128:2 * width + (p + 1) * 128]
            near = mm(q, rel_ref[...])
            for b in range(4):
                near = jnp.where(bits[b], pltpu.roll(near, 128 - (1 << b), 1), near)
            near = jnp.where(near_ok, near, 0.0)
            high = near.astype(jnp.bfloat16).astype(jnp.float32)
            both = high + pltpu.roll(near - high, 16, 1)
            both = jnp.where(one_lane, 1.0, both)
            qs = q.astype(jnp.float32) * SCALE
            xe = jnp.where(low_half, qs, both).astype(jnp.bfloat16)
            xo = jnp.where(low_half, both, qs).astype(jnp.bfloat16)
            ke = jnp.where(low_half, k, hot)
            ko = jnp.where(low_half, hot, k)
            outs = []
            for e, (xx, kk) in enumerate(((xe, ke), (xo, ko))):
                s = mm(xx, kk, NT)
                m = jnp.max(s, axis=1, keepdims=True)
                ex = jnp.exp(s - m)
                pr = (ex * (1.0 / jnp.sum(ex, axis=1, keepdims=True))).astype(jnp.bfloat16)
                prob_ref[w, 2 * p + e] = pr
                outs.append(mm(pr, v))
            out = jnp.where(low_half, outs[0], outs[1])
            ctx_ref[w * TOK:(w + 1) * TOK, p * 128:(p + 1) * 128] = out[:TOK].astype(ctx_ref.dtype)


def attention_forward(tokens, keep, gain, shift, w3, bias3, relm, hot, tab):
    rows, width = tokens.shape
    local = w3.shape[2]
    heads = local // HEAD_DIM
    step = 2 * TOK
    steps = rows // step
    full = lambda a: pl.BlockSpec(a.shape, lambda i: (0,) * a.ndim)
    return pl.pallas_call(
        fwd_kernel,
        grid=(steps,),
        in_specs=[
            pl.BlockSpec((step, width), lambda i: (i, 0)),
            pl.BlockSpec((step, 1), lambda i: (i, 0)),
            full(gain), full(shift), full(w3), full(bias3), full(relm), full(hot), full(tab),
        ],
        out_specs=[
            pl.BlockSpec((step, width), lambda i: (i, 0)),
            pl.BlockSpec((2, PADW, 3 * local), lambda i: (i, 0, 0)),
            pl.BlockSpec((2, heads, PADW, PADW), lambda i: (i, 0, 0, 0)),
            pl.BlockSpec((step, local), lambda i: (i, 0)),
        ],
        out_shape=[
            jax.ShapeDtypeStruct((rows, width), jnp.bfloat16),
            jax.ShapeDtypeStruct((2 * steps, PADW, 3 * local), jnp.bfloat16),
            jax.ShapeDtypeStruct((2 * steps, heads, PADW, PADW), jnp.bfloat16),
            jax.ShapeDtypeStruct((rows, local), jnp.float32),
        ],
        scratch_shapes=[pltpu.VMEM((step, 3 * local), jnp.float32)],
        compiler_params=pltpu.CompilerParams(vmem_limit_bytes=48 << 20),
        cost_estimate=pl.CostEstimate(
            flops=rows * 2 * (width * 3 * local + 4 * PADW * local),
            bytes_accessed=rows * width * 4 + rows * local * 12 + 2 * steps * heads * PADW * PADW * 2,
            transcendentals=rows * heads * PADW,
        ),
        name="attention_forward",
    )(tokens, keep, gain, shift, w3, bias3, relm, hot, tab)


def bwd_kernel(dctx_ref, qkv_ref, prob_ref, rel_ref, once_ref, tab_ref, dqkv_ref, drel_ref, pad_ref):
    @pl.when(pl.program_id(0) == 0)
    def _():
        drel_ref[...] = jnp.zeros_like(drel_ref)
        pad_ref[...] = jnp.zeros_like(pad_ref)

    width = dctx_ref.shape[1]
    lane = lanes()
    low_half = lane < 64
    tab = tab_ref[...]
    bits = [(tab & (1 << b)) != 0 for b in range(4)]
    once = once_ref[...]
    rel = rel_ref[...]
    for w in range(dctx_ref.shape[0] // TOK):
        pad_ref[:TOK, :] = dctx_ref[w * TOK:(w + 1) * TOK, :]
        for p in range(width // 128):
            q = qkv_ref[w, :, p * 128:(p + 1) * 128]
            k = qkv_ref[w, :, width + p * 128:width + (p + 1) * 128]
            v = qkv_ref[w, :, 2 * width + p * 128:2 * width + (p + 1) * 128]
            do32 = pad_ref[:, p * 128:(p + 1) * 128]
            do = do32.astype(jnp.bfloat16)
            qs = (q.astype(jnp.float32) * SCALE).astype(jnp.bfloat16)
            ks = (k.astype(jnp.float32) * SCALE).astype(jnp.bfloat16)
            dv, dk, dqx = [], [], []
            for e in range(2):
                mine = low_half if e == 0 else ~low_half
                pr = prob_ref[w, 2 * p + e]
                dp = mm(jnp.where(mine, do32, 0.0).astype(jnp.bfloat16), v, NT)
                dv.append(mm(pr, do, TN))
                p32 = pr.astype(jnp.float32)
                ds = (p32 * (dp - jnp.sum(dp * p32, axis=1, keepdims=True))).astype(jnp.bfloat16)
                dk.append(mm(ds, qs, TN))
                dqx.append(mm(ds, jnp.where(mine, ks, once)))
            near = jnp.where(low_half, dqx[1], dqx[0])
            for b in range(4):
                near = jnp.where(bits[b], pltpu.roll(near, 1 << b, 1), near)
            high = near.astype(jnp.bfloat16)
            rest = (near - high.astype(jnp.float32)).astype(jnp.bfloat16)
            dq = jnp.where(low_half, dqx[0], dqx[1]) + mm(high, rel, NT) + mm(rest, rel, NT)
            drel_ref[...] += mm(high, q, TN) + mm(rest, q, TN)
            for t, g in enumerate((dq, jnp.where(low_half, dk[0], dk[1]), jnp.where(low_half, dv[0], dv[1]))):
                dqkv_ref[t, w * TOK:(w + 1) * TOK, p * 128:(p + 1) * 128] = g[:TOK]


def attention_backward(dctx, qkv, prob, relm, once, tab):
    rows, local = dctx.shape
    heads = local // HEAD_DIM
    step = 2 * TOK
    steps = rows // step
    full = lambda a: pl.BlockSpec(a.shape, lambda i: (0,) * a.ndim)
    return pl.pallas_call(
        bwd_kernel,
        grid=(steps,),
        in_specs=[
            pl.BlockSpec((step, local), lambda i: (i, 0)),
            pl.BlockSpec((2, PADW, 3 * local), lambda i: (i, 0, 0)),
            pl.BlockSpec((2, heads, PADW, PADW), lambda i: (i, 0, 0, 0)),
            full(relm), full(once), full(tab),
        ],
        out_specs=[
            pl.BlockSpec((3, step, local), lambda i: (0, i, 0)),
            pl.BlockSpec((128, 128), lambda i: (0, 0)),
        ],
        out_shape=[
            jax.ShapeDtypeStruct((3, rows, local), jnp.float32),
            jax.ShapeDtypeStruct((128, 128), jnp.float32),
        ],
        scratch_shapes=[pltpu.VMEM((PADW, local), jnp.float32)],
        compiler_params=pltpu.CompilerParams(vmem_limit_bytes=48 << 20),
        cost_estimate=pl.CostEstimate(
            flops=rows * 2 * 12 * PADW * local,
            bytes_accessed=rows * local * 4 * 5 + 2 * steps * heads * PADW * PADW * 2,
            transcendentals=0,
        ),
        name="attention_backward",
    )(dctx, qkv, prob, relm, once, tab)


def split_rel(acc):
    near = acc[64:, :64] + acc[:64, 64:]
    return near[26::-1], near[58:31:-1]


def pos():
    i = lax.axis_index("dp")
    return i & 1, (i >> 1) & 1, i >> 2
PX = [(i, i ^ 1) for i in range(16)]
PY = [(i, i ^ 2) for i in range(16)]
PN = [(i, i ^ 4) for i in range(16)]
PF = [(i, i ^ 8) for i in range(16)]
pp = lambda a, perm: lax.ppermute(a, "dp", perm)
def ix(a, *ids):
    n = len(ids)
    s = lax.dynamic_slice(a, tuple(ids) + (0,) * (a.ndim - n), (1,) * n + a.shape[n:])
    return s.reshape(a.shape[n:])
def put(out, p, *ids):
    n = len(ids)
    return lax.dynamic_update_slice(out, p.reshape((1,) * n + p.shape), tuple(ids) + (0,) * p.ndim)
def rs_xy(g, x, y):
    d0 = pp(ix(g, 1 - x, 1 - y, 0), PX)
    d1 = pp(ix(g, 1 - x, 1 - y, 1), PY)
    X = ix(g, 1 - x, y); Y = ix(g, x, 1 - y)
    sx = jnp.stack([X[0], X[1] + d1]); sy = jnp.stack([Y[0] + d0, Y[1]])
    rx = pp(sx, PX); ry = pp(sy, PY)
    return [ix(g, x, y), rx, ry]
def ag_xy(c, x, y):
    rx = pp(c, PX); ry = pp(c, PY)
    d0 = pp(ry[0], PX); d1 = pp(rx[1], PY)
    out = jnp.zeros((2, 2) + c.shape, c.dtype)
    out = put(out, c, x, y); out = put(out, rx, 1 - x, y); out = put(out, ry, x, 1 - y)
    out = put(out, d0, 1 - x, 1 - y, 0); out = put(out, d1, 1 - x, 1 - y, 1)
    return out
def ar_z(terms, z):
    b0, b1 = z & 1, z >> 1
    sh = terms[0].shape
    t = [a.reshape(2, 2, -1, sh[-1]) for a in terms]
    send = sum(ix(a, 1 - b0) for a in t); keep = sum(ix(a, b0) for a in t)
    r = pp(send, PN)
    s2 = ix(keep, 1 - b1) + ix(r, 1 - b1); k2 = ix(keep, b1) + ix(r, b1)
    r2 = pp(s2, PF)
    c = k2 + r2
    o = pp(c, PF)
    h = jnp.zeros((2,) + c.shape, c.dtype)
    h = put(h, c, b1); h = put(h, o, 1 - b1)
    oh = pp(h, PN)
    w = jnp.zeros((2,) + h.shape, c.dtype)
    w = put(w, h, b0); w = put(w, oh, 1 - b0)
    return w.reshape(sh)
def allreduce(g):
    x, y, z = pos()
    R, C = g.shape
    g5 = g.reshape(2, 2, 2, R // 8, C)
    terms = rs_xy(g5, x, y)
    c = ar_z(terms, z)
    return ag_xy(c, x, y).reshape(R, C)


def row_mask(row_count, first_window):
    row_index = jnp.arange(row_count, dtype=jnp.int32)
    window = row_index // TOK + first_window
    inner = row_index % TOK
    cell = window % (GRID * GRID)
    row_pos = cell // GRID * WIN + inner // WIN
    col_pos = cell % GRID * WIN + inner % WIN
    return ((row_pos < IMG) & (col_pos < IMG)).astype(jnp.float32)[:, None]


def swap(a):
    return lax.optimization_barrier(swap_raw(a))


def swap_raw(a):
    return lax.ppermute(a, "tensor", [(0, 1), (1, 0)])


def norm_parts(x):
    mean = jnp.mean(x, axis=1, keepdims=True)
    cen = x - mean
    rstd = lax.rsqrt(jnp.mean(cen * cen, axis=1, keepdims=True) + EPS)
    return cen * rstd, rstd


def norm_back(d, hat, rstd, gain):
    dh = d * gain
    return rstd * (dh - jnp.mean(dh, axis=1, keepdims=True) - hat * jnp.mean(dh * hat, axis=1, keepdims=True))


def gelu(u):
    return 0.5 * u * (1.0 + lax.erf(u * 0.7071067811865476))


def gelu_slope(u):
    return 0.5 * (1.0 + lax.erf(u * 0.7071067811865476)) + u * jnp.exp(-0.5 * u * u) * 0.3989422804014327


def mlp_kernel(tok_ref, ctx_ref, oth_ref, wp_ref, wpo_ref, pb_ref, gain_ref, shift_ref, w1_ref, b1_ref,
               y_ref, hid_ref, pre_ref, act_ref, wpo16_ref):
    @pl.when(pl.program_id(0) == 0)
    def _():
        wpo16_ref[...] = wpo_ref[...].astype(jnp.bfloat16)

    proj = mm(ctx_ref[...].astype(jnp.bfloat16), wp_ref[...]) + mm(oth_ref[...].astype(jnp.bfloat16), wpo16_ref[...])
    y = tok_ref[...].astype(jnp.float32) + proj + pb_ref[...]
    y_ref[...] = y
    cen = y - jnp.mean(y, axis=1, keepdims=True)
    var = jnp.mean(cen * cen, axis=1, keepdims=True)
    h = (cen * lax.rsqrt(var + EPS) * gain_ref[...] + shift_ref[...]).astype(jnp.bfloat16)
    hid_ref[...] = h
    pre = mm(h, w1_ref[...]) + b1_ref[...]
    pre_ref[...] = pre
    act_ref[...] = gelu(pre).astype(jnp.bfloat16)


def mlp_forward(tokens, ctx, oth, wp, wpo, pb, gain, shift, w1, b1):
    rows, width = tokens.shape
    local, units = ctx.shape[1], w1.shape[1]
    step = 2 * TOK
    full = lambda a: pl.BlockSpec(a.shape, lambda i: (0,) * a.ndim)
    row = lambda n: pl.BlockSpec((step, n), lambda i: (i, 0))
    return pl.pallas_call(
        mlp_kernel,
        grid=(rows // step,),
        in_specs=[row(width), row(local), row(local), full(wp), full(wpo), full(pb), full(gain), full(shift), full(w1), full(b1)],
        out_specs=[row(width), row(width), row(units), row(units)],
        out_shape=[
            jax.ShapeDtypeStruct((rows, width), jnp.float32),
            jax.ShapeDtypeStruct((rows, width), jnp.bfloat16),
            jax.ShapeDtypeStruct((rows, units), jnp.float32),
            jax.ShapeDtypeStruct((rows, units), jnp.bfloat16),
        ],
        scratch_shapes=[pltpu.VMEM(wpo.shape, jnp.bfloat16)],
        compiler_params=pltpu.CompilerParams(vmem_limit_bytes=48 << 20),
        cost_estimate=pl.CostEstimate(
            flops=2 * rows * width * (2 * local + units),
            bytes_accessed=rows * (width * 8 + local * 8 + units * 6),
            transcendentals=rows * units,
        ),
        name="mlp_forward",
    )(tokens, ctx, oth, wp, wpo, pb, gain, shift, w1, b1)


def reduce_all(g):
    if lax.axis_size("dp") == 16:
        return allreduce(g)
    return lax.psum(g, "dp")


def shards(tokens, cotangent, w_qkv, qv_bias, w_proj, proj_bias, w_fc1, fc1_bias, w_fc2, fc2_bias,
           gain_one, shift_one, gain_two, shift_two, rel_h, rel_w):
    f32, bf16 = jnp.float32, jnp.bfloat16
    rows, width = tokens.shape
    local = w_qkv.shape[2]
    keep = row_mask(rows, lax.axis_index("dp") * (rows // TOK))
    g1, s1 = gain_one.astype(f32)[None], shift_one.astype(f32)[None]
    g2, s2 = gain_two.astype(f32)[None], shift_two.astype(f32)[None]
    w3 = jnp.transpose(w_qkv, (1, 0, 2))
    bias = qv_bias.astype(f32)
    bias3 = jnp.stack([bias[0], jnp.zeros_like(bias[0]), bias[1]])
    relm = rel_matrix(rel_h, rel_w)
    hot, once = key_matrix()
    tab = shift_table()
    other_proj = swap(w_proj.astype(f32))
    tok = tokens.astype(f32)

    hid1, qkv, prob, ctx = attention_forward(tokens, keep, g1, s1, w3, bias3, relm, hot, tab)
    ctx_other = swap(ctx)
    y_one, hid2, pre, act = mlp_forward(
        tokens, ctx, ctx_other, w_proj, other_proj, proj_bias.astype(f32)[None], g2, s2, w_fc1, fc1_bias.astype(f32)[None])
    ctx = ctx.astype(bf16)
    hat2, rstd2 = norm_parts(y_one)

    grad_out = keep * cotangent.astype(f32)
    grad_low = grad_out.astype(bf16)
    dw_fc2 = reduce_all(mm(act, grad_low, TN))
    d_act = mm(grad_low, w_fc2, NT)
    d_pre = (d_act * gelu_slope(pre)).astype(bf16)
    dw_fc1 = reduce_all(mm(hid2, d_pre, TN))
    d_fc1_bias = jnp.sum(d_pre.astype(f32), axis=0)
    d_fc2_bias = jnp.sum(grad_out, axis=0)

    part = mm(act, w_fc2)
    mlp = (part + swap(part)) + fc2_bias.astype(f32)
    output = (keep * (y_one + mlp)).astype(bf16)

    part = mm(d_pre, w_fc1, NT)
    d_hid2 = part + swap(part)
    d_gain_two = jnp.sum(d_hid2 * hat2, axis=0)
    d_shift_two = jnp.sum(d_hid2, axis=0)
    d_y = grad_out + norm_back(d_hid2, hat2, rstd2, g2)
    d_proj_bias = jnp.sum(d_y, axis=0)
    d_attn = d_y.astype(bf16)
    dw_proj = mm(ctx, d_attn, TN)
    d_ctx = mm(d_attn, w_proj, NT).astype(bf16).astype(f32)
    d_qkv, acc = attention_backward(d_ctx, qkv, prob, relm, once, tab)
    d_rel_h, d_rel_w = split_rel(acc)
    d_low = d_qkv.astype(bf16)
    dw_qkv = jnp.concatenate([mm(hid1, d_low[t], TN) for t in range(3)], 0)
    d_qv_bias = jnp.sum(d_low.astype(f32), axis=1)
    part = mm(d_low[0], w3[0], NT) + mm(d_low[1], w3[1], NT) + mm(d_low[2], w3[2], NT)
    d_hid1 = (part + swap(part)) * keep
    hat1, rstd1 = norm_parts(tok)
    d_tokens = (d_y + norm_back(d_hid1, hat1, rstd1, g1)).astype(bf16)
    masked = part * keep
    shared = jnp.concatenate([
        jnp.sum(masked * hat1, axis=0), jnp.sum(masked, axis=0), d_rel_h.reshape(-1), d_rel_w.reshape(-1)])
    shared = shared + swap(shared)
    small = jnp.concatenate([
        shared, d_gain_two, d_shift_two, d_proj_bias, d_fc2_bias,
        d_fc1_bias, d_qv_bias[0], d_qv_bias[2]])
    count = small.shape[0]
    small = jnp.pad(small, (0, 128 * width - count)).reshape(128, width)
    third = reduce_all(jnp.concatenate([dw_proj, small], 0))
    dw_proj, small = third[:local], third[local:].reshape(-1)[:count]
    dw_qkv = jnp.transpose(reduce_all(dw_qkv).reshape(3, width, local), (1, 0, 2))
    sizes = [width, width, rel_h.size, rel_w.size, width, width, width, width, fc1_bias.shape[0], local, local]
    cuts, at = [], 0
    for n in sizes:
        cuts.append(small[at:at + n])
        at += n
    (d_gain_one, d_shift_one, d_rel_h, d_rel_w, d_gain_two, d_shift_two, d_proj_bias, d_fc2_bias,
     d_fc1_bias, dq_bias, dv_bias) = cuts
    return (output, d_tokens, dw_qkv, jnp.stack([dq_bias, dv_bias]), dw_proj, d_proj_bias, dw_fc1, d_fc1_bias,
            dw_fc2, d_fc2_bias, d_gain_one, d_shift_one, d_gain_two, d_shift_two,
            d_rel_h.reshape(rel_h.shape), d_rel_w.reshape(rel_w.shape))


def solution(mesh):
    rows, rep = P("dp", None), P()
    ins = (rows, rows, P(None, None, "tensor"), P(None, "tensor"), P("tensor", None), rep, P(None, "tensor"),
           P("tensor"), P("tensor", None), rep, rep, rep, rep, rep, rep, rep)
    return jax.shard_map(shards, mesh=mesh, in_specs=ins, out_specs=ins, check_vma=False)
```

```python
import jax
import jax.numpy as jnp
import numpy as np
from jax import lax
from jax.experimental import pallas as pl
from jax.experimental.pallas import tpu as pltpu
from jax.sharding import PartitionSpec as P

IMG = 64
GRID = 5
HEAD_DIM = 64
WIN = 14
TOK = WIN * WIN
PADW = 208
NEG = -1e30
EPS = 1e-6
SCALE = HEAD_DIM ** -0.5
NT = (((1,), (1,)), ((), ()))
TN = (((0,), (0,)), ((), ()))
NN = (((1,), (0,)), ((), ()))
F32, BF16 = jnp.float32, jnp.bfloat16


def mm(a, b, dims=NN):
    return lax.dot_general(a, b, dims, preferred_element_type=F32)


def full(a):
    return pl.BlockSpec(a.shape, lambda i: (0,) * a.ndim)


def rel_matrix(rel_h, rel_w):
    pad = jnp.zeros((5, HEAD_DIM), rel_h.dtype)
    near = jnp.concatenate([rel_h[::-1], pad, rel_w[::-1], pad], 0)
    zero = jnp.zeros_like(near)
    return jnp.concatenate(
        [jnp.concatenate([zero, near.T], 1), jnp.concatenate([near.T, zero], 1)], 0
    )


def key_matrix():
    key = np.arange(PADW)[:, None]
    lane = np.arange(128)[None, :] % 64
    real = key < TOK
    slot = lane % 32
    once = np.where(lane < 32, key // WIN == slot, key % WIN == slot) & real & (slot < WIN)
    neg = np.where((lane == 30) & ~real, NEG, 0.0)
    once = once.astype(np.float32)
    return jnp.asarray(once, BF16), jnp.asarray(once + neg, BF16)


def shift_table():
    row = np.minimum(np.arange(PADW), TOK - 1)[:, None]
    lane = np.arange(128)[None, :] % 64
    return jnp.asarray(np.where(lane < 32, WIN - 1 - row // WIN, WIN - 1 - row % WIN), jnp.int32)


def place_table():
    row = np.arange(2 * TOK) % TOK
    out = np.zeros((2 * TOK, 128), np.float32)
    out[:, 0], out[:, 1] = row // WIN, row % WIN
    return jnp.asarray(out)


def half_lanes():
    return lax.broadcasted_iota(jnp.int32, (PADW, 128), 1) < 64


def keep_rows(place, first):
    keeps = []
    for w in range(2):
        cell = lax.rem(first + w, GRID * GRID)
        top = (IMG - lax.div(cell, GRID) * WIN).astype(F32)
        left = (IMG - lax.rem(cell, GRID) * WIN).astype(F32)
        keeps.append((top, left))
    inner = lax.broadcasted_iota(jnp.int32, (2 * TOK, 1), 0) < TOK
    top = jnp.where(inner, keeps[0][0], keeps[1][0])
    left = jnp.where(inner, keeps[0][1], keeps[1][1])
    return jnp.where((place[:, 0:1] < top) & (place[:, 1:2] < left), 1.0, 0.0)


def fwd_kernel(first_ref, x_ref, cot_ref, place_ref, gain_ref, shift_ref, w_ref, bias_ref, rel_ref, hot_ref, once_ref,
               tab_ref, hid_ref, low_ref, qkv_ref, prob_ref, ctx_ref, sum_ref, acc_ref):
    step = pl.program_id(0)
    keep = keep_rows(place_ref[...], first_ref[0] + 2 * step)
    x = x_ref[...].astype(F32)
    cen = x - jnp.mean(x, axis=1, keepdims=True)
    var = jnp.mean(cen * cen, axis=1, keepdims=True)
    h = cen * lax.rsqrt(var + EPS) * gain_ref[...] + shift_ref[...]
    h = (h * keep).astype(BF16)
    hid_ref[...] = h
    low = cot_ref[...].astype(F32) * keep
    low_ref[...] = low.astype(BF16)

    @pl.when(step == 0)
    def _():
        sum_ref[...] = jnp.zeros_like(sum_ref)

    sum_ref[...] += jnp.sum(low, axis=0, keepdims=True)
    width = w_ref.shape[2]
    for t in range(3):
        acc_ref[:, t * width:(t + 1) * width] = mm(h, w_ref[t]) + bias_ref[t:t + 1]
    low_half = half_lanes()
    lane = lax.broadcasted_iota(jnp.int32, (PADW, 128), 1)
    one_lane = lane % 64 == 30
    hot, once = hot_ref[...], once_ref[...]
    zero = jnp.zeros_like(once)
    for w in range(2):
        qkv_ref[w, :TOK, :] = acc_ref[w * TOK:(w + 1) * TOK, :].astype(BF16)
        qkv_ref[w, TOK:, :] = jnp.zeros((PADW - TOK, 3 * width), BF16)
        for p in range(width // 128):
            q = qkv_ref[w, :, p * 128:(p + 1) * 128]
            k = qkv_ref[w, :, width + p * 128:width + (p + 1) * 128] * jnp.asarray(SCALE, BF16)
            v = qkv_ref[w, :, 2 * width + p * 128:2 * width + (p + 1) * 128]
            two = mm(q, rel_ref[...])
            tab = tab_ref[...]
            near = jnp.where((tab & 8) != 0, two[:, 128:], two[:, :128])
            for b in range(3):
                near = jnp.where((tab & (1 << b)) != 0, pltpu.roll(near, 128 - (1 << b), 1), near)
            high = near.astype(BF16)
            rest = (near - high.astype(F32)).astype(BF16)
            high = jnp.where(one_lane, jnp.ones_like(high), high)
            outs = []
            for e in range(2):
                mine = low_half if e == 0 else ~low_half
                xx = jnp.concatenate([jnp.where(mine, q, high), jnp.where(mine, zero, rest)], 1)
                kk = jnp.concatenate([jnp.where(mine, k, hot), jnp.where(mine, zero, once)], 1)
                s = mm(kk, xx, NT)
                ex = jnp.exp(s - jnp.max(s, axis=0, keepdims=True))
                pr = (ex * (1.0 / jnp.sum(ex, axis=0, keepdims=True))).astype(BF16)
                prob_ref[w, 2 * p + e] = pr
                outs.append(mm(pr, v, TN))
            out = jnp.where(low_half, outs[0], outs[1])
            ctx_ref[w * TOK:(w + 1) * TOK, p * 128:(p + 1) * 128] = out[:TOK]


def attention_forward(first, tokens, cot, place, gain, shift, w3, bias3, rel2, hot, once, tab):
    rows, width = tokens.shape
    local = w3.shape[2]
    heads = local // HEAD_DIM
    step = 2 * TOK
    steps = rows // step
    row = lambda n: pl.BlockSpec((step, n), lambda i: (i, 0))
    return pl.pallas_call(
        fwd_kernel,
        grid=(steps,),
        in_specs=[
            pl.BlockSpec(memory_space=pltpu.SMEM), row(width), row(width), full(place), full(gain), full(shift),
            full(w3), full(bias3), full(rel2), full(hot), full(once), full(tab),
        ],
        out_specs=[
            row(width), row(width),
            pl.BlockSpec((2, PADW, 3 * local), lambda i: (i, 0, 0)),
            pl.BlockSpec((2, heads, PADW, PADW), lambda i: (i, 0, 0, 0)),
            row(local),
            pl.BlockSpec((1, width), lambda i: (0, 0)),
        ],
        out_shape=[
            jax.ShapeDtypeStruct((rows, width), BF16),
            jax.ShapeDtypeStruct((rows, width), BF16),
            jax.ShapeDtypeStruct((2 * steps, PADW, 3 * local), BF16),
            jax.ShapeDtypeStruct((2 * steps, heads, PADW, PADW), BF16),
            jax.ShapeDtypeStruct((rows, local), F32),
            jax.ShapeDtypeStruct((1, width), F32),
        ],
        scratch_shapes=[pltpu.VMEM((step, 3 * local), F32)],
        compiler_params=pltpu.CompilerParams(vmem_limit_bytes=48 << 20),
        cost_estimate=pl.CostEstimate(
            flops=rows * 2 * (width * 3 * local + 4 * PADW * local),
            bytes_accessed=rows * width * 8 + rows * local * 12 + 2 * steps * heads * PADW * PADW * 2,
            transcendentals=rows * heads * PADW,
        ),
        name="attention_forward",
    )(first, tokens, cot, place, gain, shift, w3, bias3, rel2, hot, once, tab)


def bwd_kernel(dctx_ref, qkv_ref, prob_ref, rel_ref, once_ref, tab_ref, dqkv_ref, drel_ref, sum_ref, pad_ref, low_ref):
    @pl.when(pl.program_id(0) == 0)
    def _():
        drel_ref[...] = jnp.zeros_like(drel_ref)
        sum_ref[...] = jnp.zeros_like(sum_ref)
        pad_ref[...] = jnp.zeros_like(pad_ref)

    width = dctx_ref.shape[1]
    low_half = half_lanes()
    once = once_ref[...]
    rel2 = rel_ref[...]
    scale = jnp.asarray(SCALE, BF16)
    for w in range(2):
        pad_ref[:TOK, :] = dctx_ref[w * TOK:(w + 1) * TOK, :]
        for p in range(width // 128):
            q = qkv_ref[w, :, p * 128:(p + 1) * 128]
            k = qkv_ref[w, :, width + p * 128:width + (p + 1) * 128] * scale
            v = qkv_ref[w, :, 2 * width + p * 128:2 * width + (p + 1) * 128]
            qs = q * scale
            do = pad_ref[:, p * 128:(p + 1) * 128].astype(BF16)
            zero = jnp.zeros_like(do)
            dv, dk, dqx = [], [], []
            for e in range(2):
                mine = low_half if e == 0 else ~low_half
                pr = prob_ref[w, 2 * p + e]
                dp = mm(v, jnp.where(mine, do, zero), NT)
                dv.append(mm(pr, do))
                p32 = pr.astype(F32)
                ds = (p32 * (dp - jnp.sum(dp * p32, axis=0, keepdims=True))).astype(BF16)
                dk.append(mm(ds, qs))
                dqx.append(mm(ds, jnp.where(mine, k, once), TN))
            near = jnp.where(low_half, dqx[1], dqx[0])
            tab = tab_ref[...]
            for b in range(4):
                near = jnp.where((tab & (1 << b)) != 0, pltpu.roll(near, 1 << b, 1), near)
            high = near.astype(BF16)
            rest = (near - high.astype(F32)).astype(BF16)
            both = jnp.concatenate([high, rest], 1)
            dq = jnp.where(low_half, dqx[0], dqx[1]) + mm(both, rel2, NT)
            drel_ref[...] += mm(q, both, TN)
            for t, g in enumerate((dq, jnp.where(low_half, dk[0], dk[1]), jnp.where(low_half, dv[0], dv[1]))):
                low_ref[t, w * TOK:(w + 1) * TOK, p * 128:(p + 1) * 128] = g[:TOK]
    for t in range(3):
        g = low_ref[t].astype(BF16)
        dqkv_ref[t] = g
        sum_ref[t:t + 1, :] += jnp.sum(g.astype(F32), axis=0, keepdims=True)


def bwd_more_kernel(dctx_ref, qkv_ref, prob_ref, rel_ref, once_ref, tab_ref, _, *rest):
    bwd_kernel(dctx_ref, qkv_ref, prob_ref, rel_ref, once_ref, tab_ref, *rest)


def attention_backward(dctx, qkv, prob, rel2, once, tab, part, parts, done=None):
    rows, local = dctx.shape
    heads = local // HEAD_DIM
    step = 2 * TOK
    steps = rows // step // parts
    at = part * steps
    more = [] if done is None else [done]
    kernel = bwd_kernel if done is None else bwd_more_kernel
    return pl.pallas_call(
        kernel,
        grid=(steps,),
        input_output_aliases={} if done is None else {6: 0},
        in_specs=[
            pl.BlockSpec((step, local), lambda i: (i + at, 0)),
            pl.BlockSpec((2, PADW, 3 * local), lambda i: (i + at, 0, 0)),
            pl.BlockSpec((2, heads, PADW, PADW), lambda i: (i + at, 0, 0, 0)),
            full(rel2), full(once), full(tab),
        ] + [pl.BlockSpec(memory_space=pl.ANY) for _ in more],
        out_specs=[
            pl.BlockSpec((3, step, local), lambda i: (0, i + at, 0)),
            pl.BlockSpec((128, 256), lambda i: (0, 0)),
            pl.BlockSpec((8, local), lambda i: (0, 0)),
        ],
        out_shape=[
            jax.ShapeDtypeStruct((3, rows, local), BF16),
            jax.ShapeDtypeStruct((128, 256), F32),
            jax.ShapeDtypeStruct((8, local), F32),
        ],
        scratch_shapes=[pltpu.VMEM((PADW, local), F32), pltpu.VMEM((3, step, local), F32)],
        compiler_params=pltpu.CompilerParams(vmem_limit_bytes=48 << 20),
        cost_estimate=pl.CostEstimate(
            flops=steps * step * 2 * 12 * PADW * local,
            bytes_accessed=steps * step * local * 4 * 5 + 2 * steps * heads * PADW * PADW * 2,
            transcendentals=0,
        ),
        name="attention_backward",
    )(dctx, qkv, prob, rel2, once, tab, *more)


def split_rel(acc):
    acc = acc[:, :128] + acc[:, 128:]
    near = (acc[:64, 64:] + acc[64:, :64]).T
    return near[26::-1], near[58:31:-1]


def row_spec(n):
    return pl.BlockSpec((2 * TOK, n), lambda i: (i, 0))


def accumulate(ref, rows):
    @pl.when(pl.program_id(0) == 0)
    def _():
        ref[...] = jnp.zeros_like(ref)

    for i, r in enumerate(rows):
        ref[i:i + 1, :] += jnp.sum(r, axis=0, keepdims=True)


def mlp_half(h, low, w1, b1, w2, act_ref, pre_ref, sum_ref):
    u = mm(h, w1) + b1
    cdf = 0.5 * (1.0 + lax.erf(u * 0.7071067811865476))
    act_ref[...] = (u * cdf).astype(BF16)
    slope = cdf + u * jnp.exp(-0.5 * u * u) * 0.3989422804014327
    d = (mm(low, w2, NT) * slope).astype(BF16)
    pre_ref[...] = d
    accumulate(sum_ref, [d.astype(F32)])


def mlp_first_kernel(tok_ref, ctx_ref, oth_ref, low_ref, wp_ref, wpo_ref, pb_ref, gain_ref, shift_ref, w1_ref, b1_ref,
                     w2_ref, y_ref, hid_ref, act_ref, pre_ref, sum_ref, wpo16_ref):
    @pl.when(pl.program_id(0) == 0)
    def _():
        wpo16_ref[...] = wpo_ref[...].astype(BF16)

    proj = mm(ctx_ref[...].astype(BF16), wp_ref[...]) + mm(oth_ref[...].astype(BF16), wpo16_ref[...])
    y = tok_ref[...].astype(F32) + proj + pb_ref[...]
    y_ref[...] = y
    cen = y - jnp.mean(y, axis=1, keepdims=True)
    var = jnp.mean(cen * cen, axis=1, keepdims=True)
    h = (cen * lax.rsqrt(var + EPS) * gain_ref[...] + shift_ref[...]).astype(BF16)
    hid_ref[...] = h
    mlp_half(h, low_ref[...], w1_ref[...], b1_ref[...], w2_ref[...], act_ref, pre_ref, sum_ref)


def mlp_second_kernel(hid_ref, low_ref, w1_ref, b1_ref, w2_ref, act_ref, pre_ref, sum_ref):
    mlp_half(hid_ref[...], low_ref[...], w1_ref[...], b1_ref[...], w2_ref[...], act_ref, pre_ref, sum_ref)


def half_weight_specs(width, units, part):
    return [
        pl.BlockSpec((width, units), lambda i: (0, part)),
        pl.BlockSpec((1, units), lambda i: (0, part)),
        pl.BlockSpec((units, width), lambda i: (part, 0)),
    ]


def mlp_first(tokens, ctx, oth, low, wp, wpo, pb, gain, shift, w1, b1, w2):
    rows, width = tokens.shape
    local, units = ctx.shape[1], w1.shape[1] // 2
    return pl.pallas_call(
        mlp_first_kernel,
        grid=(rows // (2 * TOK),),
        in_specs=[row_spec(width), row_spec(local), row_spec(local), row_spec(width), full(wp), full(wpo), full(pb),
                  full(gain), full(shift)] + half_weight_specs(width, units, 0),
        out_specs=[row_spec(width), row_spec(width), row_spec(units), row_spec(units),
                   pl.BlockSpec((1, units), lambda i: (0, 0))],
        out_shape=[
            jax.ShapeDtypeStruct((rows, width), F32),
            jax.ShapeDtypeStruct((rows, width), BF16),
            jax.ShapeDtypeStruct((rows, units), BF16),
            jax.ShapeDtypeStruct((rows, units), BF16),
            jax.ShapeDtypeStruct((1, units), F32),
        ],
        scratch_shapes=[pltpu.VMEM(wpo.shape, BF16)],
        compiler_params=pltpu.CompilerParams(vmem_limit_bytes=48 << 20),
        cost_estimate=pl.CostEstimate(
            flops=2 * rows * width * (2 * local + 2 * units),
            bytes_accessed=rows * (width * 10 + local * 8 + units * 4), transcendentals=rows * units),
        name="mlp_first",
    )(tokens, ctx, oth, low, wp, wpo, pb, gain, shift, w1, b1, w2)


def mlp_second(hid, low, w1, b1, w2):
    rows, width = hid.shape
    units = w1.shape[1] // 2
    return pl.pallas_call(
        mlp_second_kernel,
        grid=(rows // (2 * TOK),),
        in_specs=[row_spec(width), row_spec(width)] + half_weight_specs(width, units, 1),
        out_specs=[row_spec(units), row_spec(units), pl.BlockSpec((1, units), lambda i: (0, 0))],
        out_shape=[
            jax.ShapeDtypeStruct((rows, units), BF16),
            jax.ShapeDtypeStruct((rows, units), BF16),
            jax.ShapeDtypeStruct((1, units), F32),
        ],
        compiler_params=pltpu.CompilerParams(vmem_limit_bytes=48 << 20),
        cost_estimate=pl.CostEstimate(
            flops=2 * rows * width * 2 * units, bytes_accessed=rows * (width * 4 + units * 4),
            transcendentals=rows * units),
        name="mlp_second",
    )(hid, low, w1, b1, w2)


def norm_back(d, hat, rstd, gain):
    dh = d * gain
    return rstd * (dh - jnp.mean(dh, axis=1, keepdims=True) - hat * jnp.mean(dh * hat, axis=1, keepdims=True))


def norm_parts(x):
    cen = x - jnp.mean(x, axis=1, keepdims=True)
    rstd = lax.rsqrt(jnp.mean(cen * cen, axis=1, keepdims=True) + EPS)
    return cen * rstd, rstd


def norm_two_kernel(part_ref, oth_ref, y_ref, low_ref, gain_ref, wp_ref, dy_ref, attn_ref, dctx_ref, sum_ref):
    d = part_ref[...] + oth_ref[...]
    hat, rstd = norm_parts(y_ref[...])
    dy = low_ref[...].astype(F32) + norm_back(d, hat, rstd, gain_ref[...])
    dy_ref[...] = dy
    low = dy.astype(BF16)
    attn_ref[...] = low
    dctx_ref[...] = mm(low, wp_ref[...], NT)
    accumulate(sum_ref, [d * hat, d, dy])


def norm_two_back(part, oth, y, low, gain, wp):
    rows, width = y.shape
    local = wp.shape[0]
    return pl.pallas_call(
        norm_two_kernel,
        grid=(rows // (2 * TOK),),
        in_specs=[row_spec(width)] * 4 + [full(gain), full(wp)],
        out_specs=[row_spec(width), row_spec(width), row_spec(local), pl.BlockSpec((8, width), lambda i: (0, 0))],
        out_shape=[
            jax.ShapeDtypeStruct((rows, width), F32),
            jax.ShapeDtypeStruct((rows, width), BF16),
            jax.ShapeDtypeStruct((rows, local), F32),
            jax.ShapeDtypeStruct((8, width), F32),
        ],
        compiler_params=pltpu.CompilerParams(vmem_limit_bytes=48 << 20),
        cost_estimate=pl.CostEstimate(
            flops=2 * rows * width * local, bytes_accessed=rows * (width * 20 + local * 4), transcendentals=0),
        name="norm_two_back",
    )(part, oth, y, low, gain, wp)


def norm_one_kernel(first_ref, part_ref, oth_ref, tok_ref, dy_ref, place_ref, gain_ref, dtok_ref, sum_ref):
    keep = keep_rows(place_ref[...], first_ref[0] + 2 * pl.program_id(0))
    d = (part_ref[...] + oth_ref[...]) * keep
    hat, rstd = norm_parts(tok_ref[...].astype(F32))
    dtok_ref[...] = (dy_ref[...] + norm_back(d, hat, rstd, gain_ref[...])).astype(BF16)
    accumulate(sum_ref, [d * hat, d])


def norm_one_back(first, part, oth, tokens, dy, place, gain):
    rows, width = tokens.shape
    return pl.pallas_call(
        norm_one_kernel,
        grid=(rows // (2 * TOK),),
        in_specs=[pl.BlockSpec(memory_space=pltpu.SMEM)] + [row_spec(width)] * 4 + [full(place), full(gain)],
        out_specs=[row_spec(width), pl.BlockSpec((8, width), lambda i: (0, 0))],
        out_shape=[jax.ShapeDtypeStruct((rows, width), BF16), jax.ShapeDtypeStruct((8, width), F32)],
        compiler_params=pltpu.CompilerParams(vmem_limit_bytes=48 << 20),
        cost_estimate=pl.CostEstimate(flops=rows * width * 20, bytes_accessed=rows * width * 16, transcendentals=0),
        name="norm_one_back",
    )(first, part, oth, tokens, dy, place, gain)


def output_kernel(first_ref, part_ref, oth_ref, y_ref, place_ref, bias_ref, out_ref):
    keep = keep_rows(place_ref[...], first_ref[0] + 2 * pl.program_id(0))
    mlp = (part_ref[...] + oth_ref[...]) + bias_ref[...]
    out_ref[...] = (keep * (y_ref[...] + mlp)).astype(BF16)


def block_output(first, part, oth, y, place, bias):
    rows, width = y.shape
    return pl.pallas_call(
        output_kernel,
        grid=(rows // (2 * TOK),),
        in_specs=[pl.BlockSpec(memory_space=pltpu.SMEM)] + [row_spec(width)] * 3 + [full(place), full(bias)],
        out_specs=row_spec(width),
        out_shape=jax.ShapeDtypeStruct((rows, width), BF16),
        compiler_params=pltpu.CompilerParams(vmem_limit_bytes=48 << 20),
        cost_estimate=pl.CostEstimate(flops=rows * width * 4, bytes_accessed=rows * width * 14, transcendentals=0),
        name="block_output",
    )(first, part, oth, y, place, bias)


def wait_for(arrays, token):
    return arrays if token is None else lax.optimization_barrier((arrays, token))[0]


def hold(arrays):
    return lax.optimization_barrier(arrays)


def send(a, stride):
    n = lax.axis_size("dp")
    return lax.ppermute(a, "dp", [(i, i ^ stride) for i in range(n)])


def pick(a, *ids):
    n = len(ids)
    return lax.dynamic_slice(a, tuple(ids) + (0,) * (a.ndim - n), (1,) * n + a.shape[n:]).reshape(a.shape[n:])


def put(out, piece, *ids):
    n = len(ids)
    return lax.dynamic_update_slice(out, piece.reshape((1,) * n + piece.shape), tuple(ids) + (0,) * piece.ndim)


def both(b, a, c):
    out = jnp.zeros((2,) + a.shape, a.dtype)
    return put(put(out, a, b), c, 1 - b)


class Plane:
    def __init__(self, g, bits, home):
        self.x, self.y, self.b0, self.b1 = bits
        self.rows, self.cols = g.shape
        self.home = home
        self.live = self.start(g)

    def start(self, g):
        return (g.reshape(2, 2, 2, self.rows // 8, self.cols),)

    def step(self, name, token):
        self.live, token = getattr(self, name)(*wait_for(self.live, token))
        return token

    def s1(self, g):
        x, y = self.x, self.y
        d0, d1 = hold((pick(g, 1 - x, 1 - y, 0), pick(g, 1 - x, 1 - y, 1)))
        return (g, send(d0, 1), send(d1, 2)), d0

    def s2(self, g, d0, d1):
        x, y = self.x, self.y
        to_x, to_y = pick(g, 1 - x, y), pick(g, x, 1 - y)
        to_x = jnp.concatenate([to_x[:1], to_x[1:] + d1[None]])
        to_y = jnp.concatenate([to_y[:1] + d0[None], to_y[1:]])
        to_x, to_y = hold((to_x, to_y))
        return (g, send(to_x, 1), send(to_y, 2)), to_x

    def z1(self, g, rx, ry):
        own = pick(g, self.x, self.y)
        b = self.b0
        out = pick(own, 1 - b) + pick(rx, 1 - b) + pick(ry, 1 - b)
        keep = pick(own, b) + pick(rx, b) + pick(ry, b)
        out, keep = hold((out, keep))
        return (keep, send(out, 4)), out

    def split(self, a):
        h, c = a.shape
        return a.reshape(2, h // 2, c) if h % 16 == 0 else a.reshape(h, 2, c // 2).transpose(1, 0, 2)

    def z2(self, keep, r):
        keep, r, b = self.split(keep), self.split(r), self.b1
        out = pick(keep, 1 - b) + pick(r, 1 - b)
        keep = pick(keep, b) + pick(r, b)
        out, keep = hold((out, keep))
        return (keep, send(out, 8)), out

    def z3(self, keep, r):
        c = hold(keep + r)
        return (c, send(c, 8)), c

    def z4(self, c, o):
        h = both(self.b1, c, o)
        n = self.rows // 8
        h = h.reshape(n, self.cols) if n % 16 == 0 else h.transpose(1, 0, 2).reshape(n, self.cols)
        h = hold(h)
        return (h, send(h, 4)), h

    def g1(self, h, o):
        w = hold(both(self.b0, h, o))
        return (w, send(w, 1), send(w, 2)), w

    def g2(self, w, rx, ry):
        a, b = hold((ry[0], rx[1]))
        return (w, rx, ry, send(a, 1), send(b, 2)), a

    def gather(self, out, w, rx, ry, d0, d1, row0, col0):
        x, y = self.x, self.y
        slab = w.shape[0] * w.shape[1]
        for piece, px, py, off in ((w, x, y, 0), (rx, 1 - x, y, 0), (ry, x, 1 - y, 0),
                                   (d0, 1 - x, 1 - y, 0), (d1, 1 - x, 1 - y, slab // 2)):
            piece = piece.reshape(-1, piece.shape[-1])
            out = lax.dynamic_update_slice(out, piece, (row0 + (2 * px + py) * slab + off, col0))
        return out

    def end(self, w, rx, ry, d0, d1):
        bufs, name, row0, col0 = self.home
        bufs[name] = hold(self.gather(bufs[name], w, rx, ry, d0, d1, row0, col0))
        return (), bufs[name]


class Column(Plane):
    def start(self, g):
        return (g.reshape(2, 2, self.rows // 4, self.cols),)

    def z1(self, g):
        out = hold(pick(g, 1 - self.b0))
        return (g, send(out, 4)), out

    def z2(self, g, r):
        b0, b1 = self.b0, self.b1
        out = pick(g, b0, 1 - b1) + pick(r, 1 - b1)
        keep = pick(g, b0, b1) + pick(r, b1)
        out, keep = hold((out, keep))
        return (keep, send(out, 8)), out

    def s1(self, keep, r):
        return Plane.s1(self, hold((keep + r).reshape(2, 2, 2, self.rows // 32, self.cols)))

    def g1(self, g, rx, ry):
        w = hold(pick(g, self.x, self.y) + rx + ry)
        return (w, send(w, 1), send(w, 2)), w

    def z3(self, w, rx, ry, d0, d1):
        c = jnp.zeros((self.rows // 4, self.cols), w.dtype)
        c = hold(self.gather(c, w, rx, ry, d0, d1, 0, 0))
        return (c, send(c, 8)), c

    def z4(self, c, o):
        h = hold(both(self.b1, c, o))
        return (h, send(h, 4)), h

    def end(self, h, o):
        bufs, name, row0, col0 = self.home
        n = self.rows // 2
        for piece, b in ((h, self.b0), (o, 1 - self.b0)):
            bufs[name] = lax.dynamic_update_slice(bufs[name], piece.reshape(n, self.cols), (row0 + b * n, col0))
        bufs[name] = hold(bufs[name])
        return (), bufs[name]


def swap(a):
    return lax.ppermute(a, "tensor", [(0, 1), (1, 0)])


class Block:
    def __init__(self, args):
        (self.tokens, self.cot, w_qkv, qv_bias, self.w_proj, proj_bias, self.w_fc1, fc1_bias, self.w_fc2, fc2_bias,
         gain_one, shift_one, gain_two, shift_two, rel_h, rel_w) = args
        self.rows, self.width = self.tokens.shape
        self.local = w_qkv.shape[2]
        self.units = self.w_fc1.shape[1] // 2
        self.rel_shape = rel_h.shape
        index = lax.axis_index("dp")
        self.first = jnp.reshape(index * (self.rows // TOK), (1,)).astype(jnp.int32)
        self.bits = tuple((index >> b) & 1 for b in range(4))
        line = lambda v: v.astype(F32)[None]
        self.g1, self.s1, self.g2, self.s2 = line(gain_one), line(shift_one), line(gain_two), line(shift_two)
        self.pb, self.b1, self.b2 = line(proj_bias), line(fc1_bias), line(fc2_bias)
        self.w3 = jnp.transpose(w_qkv, (1, 0, 2))
        bias = qv_bias.astype(F32)
        self.bias3 = jnp.stack([bias[0], jnp.zeros_like(bias[0]), bias[1]])
        relm = rel_matrix(rel_h, rel_w)
        self.rel_fwd = jnp.concatenate([relm, jnp.roll(relm, -8, axis=1)], 1)
        self.rel_bwd = jnp.concatenate([relm, relm], 1)
        self.once, self.hot = key_matrix()
        self.tab, self.spots = shift_table(), place_table()
        self.bufs = {
            "fc2": jnp.zeros((2 * self.units, self.width), F32),
            "fc1": jnp.zeros((self.width, 2 * self.units), F32),
            "qkv": jnp.zeros((3 * self.width, self.local), F32),
            "rest": jnp.zeros((self.local + 64, self.width), F32),
        }
        self.grads = {}

    def K1(self, token):
        other = swap(self.w_proj.astype(F32))
        self.hid1, self.low, self.qkv, self.prob, self.ctx, self.d_fc2_bias = attention_forward(
            self.first, self.tokens, self.cot, self.spots, self.g1, self.s1, self.w3, self.bias3, self.rel_fwd,
            self.hot, self.once, self.tab)
        self.ctx_other, self.proj_other = swap(self.ctx), other
        return self.ctx

    def K2a(self, token):
        ctx = wait_for(self.ctx, token)
        self.y, self.hid2, self.act0, self.pre0, self.sum0 = mlp_first(
            self.tokens, ctx, self.ctx_other, self.low, self.w_proj, self.proj_other, self.pb, self.g2, self.s2,
            self.w_fc1, self.b1, self.w_fc2)
        return self.hid2

    def K2b(self, token):
        hid = wait_for(self.hid2, token)
        self.act1, self.pre1, self.sum1 = mlp_second(hid, self.low, self.w_fc1, self.b1, self.w_fc2)
        return self.act1

    def grad(self, name, a, b, token):
        a = wait_for(a, token)
        self.grads[name] = hold(mm(a, b, TN))
        return self.grads[name]

    def dw2a(self, token):
        return self.grad("A0", self.act0, self.low, token)

    def dw2b(self, token):
        return self.grad("A1", self.act1, self.low, token)

    def dw2(self, token):
        low = wait_for(self.low, token)
        self.grads["A"] = hold(jnp.concatenate([mm(self.act0, low, TN), mm(self.act1, low, TN)], 0))
        return self.grads["A"]

    def dw1a(self, token):
        return self.grad("B0", self.hid2, self.pre0, token)

    def dw1b(self, token):
        return self.grad("B1", self.hid2, self.pre1, token)

    def dh2(self, token):
        pre = wait_for(self.pre0, token)
        n = self.units
        part = hold(mm(pre, self.w_fc1[:, :n], NT) + mm(self.pre1, self.w_fc1[:, n:], NT))
        self.dh2_part, self.dh2_other = part, swap(part)
        return part

    def fc2(self, token):
        act = wait_for(self.act0, token)
        n = self.units
        part = hold(mm(act, self.w_fc2[:n]) + mm(self.act1, self.w_fc2[n:]))
        self.fc2_part, self.fc2_other = part, swap(part)
        return part

    def K3(self, token):
        y = wait_for(self.y, token)
        self.dy, self.d_attn, self.dctx, self.sum_two = norm_two_back(
            self.dh2_part, self.dh2_other, y, self.low, self.g2, self.w_proj)
        return self.dctx

    def K4a(self, token):
        dctx = wait_for(self.dctx, token)
        self.dqkv, self.acc0, self.bias0 = attention_backward(
            dctx, self.qkv, self.prob, self.rel_bwd, self.once, self.tab, 0, 2)
        return self.acc0

    def K4b(self, token):
        dctx = wait_for(self.dctx, token)
        self.dqkv, acc, bias = attention_backward(
            dctx, self.qkv, self.prob, self.rel_bwd, self.once, self.tab, 1, 2, self.dqkv)
        self.acc = hold(self.acc0 + acc)
        self.acc_other = swap(self.acc)
        self.bias_qv = self.bias0 + bias
        return self.acc

    def dwq(self, token):
        hid = wait_for(self.hid1, token)
        self.grads["C"] = hold(jnp.concatenate([mm(hid, self.dqkv[t], TN) for t in range(3)], 0))
        return self.grads["C"]

    def dh1(self, token):
        d = wait_for(self.dqkv, token)
        part = hold(mm(d[0], self.w3[0], NT) + mm(d[1], self.w3[1], NT) + mm(d[2], self.w3[2], NT))
        self.dh1_part, self.dh1_other = part, swap(part)
        return part

    def dproj(self, token):
        attn = wait_for(self.d_attn, token)
        self.d_proj = hold(mm(self.ctx.astype(BF16), attn, TN))
        return self.d_proj

    def K5(self, token):
        dy = wait_for(self.dy, token)
        self.d_tokens, sum_one = norm_one_back(
            self.first, self.dh1_part, self.dh1_other, self.tokens, dy, self.spots, self.g1)
        rel_h, rel_w = split_rel(self.acc + self.acc_other)
        self.small = [
            sum_one[0], sum_one[1], self.sum_two[0], self.sum_two[1], self.sum_two[2], self.d_fc2_bias[0],
            self.sum0[0], self.sum1[0], self.bias_qv[0], self.bias_qv[2], rel_h.reshape(-1), rel_w.reshape(-1)]
        flat = jnp.concatenate(self.small)
        flat = jnp.pad(flat, (0, 64 * self.width - flat.shape[0])).reshape(64, self.width)
        self.flat = flat
        return self.d_tokens

    def K6(self, token):
        y = wait_for(self.y, token)
        self.output = block_output(self.first, self.fc2_part, self.fc2_other, y, self.spots, self.b2)
        return self.output

    def rest(self):
        self.grads["D"] = jnp.concatenate([self.d_proj, self.flat], 0)

    def results(self):
        n = self.local
        cuts, at = [], 0
        flat = self.bufs["rest"][n:].reshape(-1)
        for a in self.small:
            cuts.append(flat[at:at + a.shape[0]])
            at += a.shape[0]
        gain1, shift1, gain2, shift2, projb, fc2b, b1a, b1b, qb, vb, rel_h, rel_w = cuts
        dw_qkv = jnp.transpose(self.bufs["qkv"].reshape(3, self.width, n), (1, 0, 2))
        return (self.output, self.d_tokens, dw_qkv, jnp.stack([qb, vb]), self.bufs["rest"][:n], projb,
                self.bufs["fc1"], jnp.concatenate([b1a, b1b]), self.bufs["fc2"], fc2b, gain1, shift1, gain2, shift2,
                rel_h.reshape(self.rel_shape), rel_w.reshape(self.rel_shape))


def homes(block):
    u = block.units
    return {"A": ("fc2", 0, 0), "A0": ("fc2", 0, 0), "A1": ("fc2", u, 0), "B0": ("fc1", 0, 0), "B1": ("fc1", 0, u),
            "C": ("qkv", 0, 0), "D": ("rest", 0, 0)}


ORDER = (
    "K1", "K2a", "K2b", "dw2", "A.s1", "dw1b", "dw1a", "dh2", "B1.s1", "B0.z1", "A.s2", "K3", "K4a", "B1.s2", "B0.z2", "A.z1", "K4b", "dwq", "C.s1", "B1.z1", "A.z2",
    "dh1", "B0.s1", "B1.z2", "C.s2", "A.z3", "K5", "dproj", "B0.s2", "B1.z3", "D.s1", "A.z4", "C.z1", "B0.g1", "D.s2", "B0.g2", "A.g1", "B1.z4", "D.z1", "C.z2",
    "fc2", "B1.g1", "D.z2", "C.z3", "D.z3", "B0.z3", "A.g2", "D.z4", "B1.g2", "C.z4", "D.g1", "C.g1", "B0.z4", "D.g2", "K6", "B1.end", "A.end", "C.g2", "D.end",
    "B0.end", "C.end",
)
COLUMNS = ('B0',)


def shards(*args):
    block = Block(args)
    where = homes(block)
    token, sums, ordered = None, {}, lax.axis_size("dp") == 16
    for item in ORDER:
        if "." not in item:
            token = getattr(block, item)(token)
            continue
        if not ordered:
            continue
        name, step = item.split(".")
        if name not in sums:
            if name == "D":
                block.rest()
            kind = Column if name in COLUMNS else Plane
            sums[name] = kind(block.grads[name], block.bits, (block.bufs,) + where[name])
        token = sums[name].step(step, token)
    if not ordered:
        block.rest()
        total = lax.psum(block.grads, "dp")
        for name, g in total.items():
            buf, row, col = where[name]
            block.bufs[buf] = lax.dynamic_update_slice(block.bufs[buf], g, (row, col))
    return block.results()


def solution(mesh):
    rows, rep = P("dp", None), P()
    ins = (rows, rows, P(None, None, "tensor"), P(None, "tensor"), P("tensor", None), rep, P(None, "tensor"),
           P("tensor"), P("tensor", None), rep, rep, rep, rep, rep, rep, rep)
    return jax.shard_map(shards, mesh=mesh, in_specs=ins, out_specs=ins, check_vma=False)
```

```python
import functools
import jax
import jax.numpy as jnp
from jax import lax
from jax.experimental import pallas as pl
from jax.experimental.pallas import tpu as pltpu
from jax.sharding import PartitionSpec as P

IMG = 64
GRID = 5
HEAD_DIM = 64
WIN = 14
TOK = WIN * WIN
PADW = 208
NEG = -1e30
EPS = 1e-6
SCALE = HEAD_DIM ** -0.5
NT = (((1,), (1,)), ((), ()))
TN = (((0,), (0,)), ((), ()))
NN = (((1,), (0,)), ((), ()))
F32, BF16 = jnp.float32, jnp.bfloat16
UNIT = 1
STEP = 1


def cost(amount):
    return pl.CostEstimate(flops=int(amount * UNIT), bytes_accessed=1, transcendentals=0)


def step_cost():
    return pl.CostEstimate(flops=STEP, bytes_accessed=1, transcendentals=0)


def mm(a, b, dims=NN):
    return lax.dot_general(a, b, dims, preferred_element_type=F32)


def full(a):
    return pl.BlockSpec(a.shape, lambda i: (0,) * a.ndim)


def iota(shape, axis):
    return lax.broadcasted_iota(jnp.int32, shape, axis)


def over_win(r):
    return jnp.floor((r.astype(F32) + 0.5) * (1.0 / WIN)).astype(jnp.int32)


def rel_tables(rel_h, rel_w, shift):
    slots = 2 * WIN - 1
    halves = []
    for base in (64, 0):
        sums = 0.0
        for at, rel in ((0, rel_h), (32, rel_w)):
            lane, offset = iota((slots, 128), 1), iota((slots, 128), 0)
            hot = ((lane - base - at + shift) == (slots - 1 - offset)) & (lane >= base) & (lane < base + 64)
            sums = sums + mm(rel, jnp.where(hot, 1.0, 0.0).astype(BF16), TN)
        halves.append(sums.astype(BF16))
    return jnp.concatenate(halves, 0)


def key_table(mask):
    key, lane = iota((PADW, 128), 0), iota((PADW, 128), 1) & 63
    row = over_win(key)
    slot = lane & 31
    want = jnp.where(lane < 32, row, key - row * WIN)
    hot = (want == slot) & (key < TOK) & (slot < WIN)
    return jnp.where(hot, 1.0, jnp.where((lane == 30) & (key >= TOK), mask, 0.0)).astype(BF16)


def shift_table():
    row, lane = jnp.minimum(iota((PADW, 128), 0), TOK - 1), iota((PADW, 128), 1) & 63
    high = over_win(row)
    return WIN - 1 - jnp.where(lane < 32, high, row - high * WIN)


def half_lanes():
    return lax.broadcasted_iota(jnp.int32, (PADW, 128), 1) < 64


def keep_rows(first):
    r = iota((2 * TOK, 1), 0)
    second = r >= TOK
    r = jnp.where(second, r - TOK, r)
    row = over_win(r)
    col = r - row * WIN
    limits = []
    for w in range(2):
        cell = lax.rem(first + w, GRID * GRID)
        limits.append((IMG - lax.div(cell, GRID) * WIN, IMG - lax.rem(cell, GRID) * WIN))
    top = jnp.where(second, limits[1][0], limits[0][0])
    left = jnp.where(second, limits[1][1], limits[0][1])
    return jnp.where((row < top) & (col < left), 1.0, 0.0)


def fwd_kernel(first_ref, x_ref, cot_ref, gain_ref, shift_ref, w_ref, bias_ref, relh_ref, relw_ref,
               hid_ref, low_ref, qkv_ref, prob_ref, ctx_ref, sum_ref, acc_ref, rel_ref, hot_ref, once_ref, tab_ref):
    step = pl.program_id(0)

    @pl.when(step == 0)
    def _():
        sum_ref[...] = jnp.zeros_like(sum_ref)
        rel_ref[:, :128] = rel_tables(relh_ref[...], relw_ref[...], 0)
        rel_ref[:, 128:] = rel_tables(relh_ref[...], relw_ref[...], 8)
        hot_ref[...], once_ref[...], tab_ref[...] = key_table(NEG), key_table(0.0), shift_table()

    keep = keep_rows(first_ref[0] + 2 * step)
    x = x_ref[...].astype(F32)
    cen = x - jnp.mean(x, axis=1, keepdims=True)
    var = jnp.mean(cen * cen, axis=1, keepdims=True)
    h = cen * lax.rsqrt(var + EPS) * gain_ref[...].astype(F32) + shift_ref[...].astype(F32)
    h = (h * keep).astype(BF16)
    hid_ref[...] = h
    low = cot_ref[...].astype(F32) * keep
    low_ref[...] = low.astype(BF16)

    sum_ref[...] += jnp.sum(low, axis=0, keepdims=True)
    width = w_ref.shape[2]
    for t in range(3):
        part = mm(h, w_ref[t])
        acc_ref[:, t * width:(t + 1) * width] = part if t == 1 else part + bias_ref[t // 2:t // 2 + 1, :].astype(F32)
    low_half = half_lanes()
    lane = lax.broadcasted_iota(jnp.int32, (PADW, 128), 1)
    one_lane = lane % 64 == 30
    hot, once = hot_ref[...], once_ref[...]
    zero = jnp.zeros_like(once)
    for w in range(2):
        qkv_ref[w, :TOK, :] = acc_ref[w * TOK:(w + 1) * TOK, :].astype(BF16)
        qkv_ref[w, TOK:, :] = jnp.zeros((PADW - TOK, 3 * width), BF16)
        for p in range(width // 128):
            q = qkv_ref[w, :, p * 128:(p + 1) * 128]
            k = qkv_ref[w, :, width + p * 128:width + (p + 1) * 128] * jnp.asarray(SCALE, BF16)
            v = qkv_ref[w, :, 2 * width + p * 128:2 * width + (p + 1) * 128]
            two = mm(q, rel_ref[...])
            tab = tab_ref[...]
            near = jnp.where((tab & 8) != 0, two[:, 128:], two[:, :128])
            for b in range(3):
                near = jnp.where((tab & (1 << b)) != 0, pltpu.roll(near, 128 - (1 << b), 1), near)
            high = near.astype(BF16)
            rest = (near - high.astype(F32)).astype(BF16)
            high = jnp.where(one_lane, jnp.ones_like(high), high)
            outs = []
            for e in range(2):
                mine = low_half if e == 0 else ~low_half
                xx = jnp.concatenate([jnp.where(mine, q, high), jnp.where(mine, zero, rest)], 1)
                kk = jnp.concatenate([jnp.where(mine, k, hot), jnp.where(mine, zero, once)], 1)
                s = mm(kk, xx, NT)
                ex = jnp.exp(s - jnp.max(s, axis=0, keepdims=True))
                pr = (ex * (1.0 / jnp.sum(ex, axis=0, keepdims=True))).astype(BF16)
                prob_ref[w, 2 * p + e] = pr
                outs.append(mm(pr, v, TN))
            out = jnp.where(low_half, outs[0], outs[1])
            ctx_ref[w * TOK:(w + 1) * TOK, p * 128:(p + 1) * 128] = out[:TOK]


def attention_forward(first, tokens, cot, gain, shift, w3, bias, rel_h, rel_w):
    rows, width = tokens.shape
    local = w3.shape[2]
    heads = local // HEAD_DIM
    step = 2 * TOK
    steps = rows // step
    row = lambda n: pl.BlockSpec((step, n), lambda i: (i, 0))
    return pl.pallas_call(
        fwd_kernel,
        grid=(steps,),
        in_specs=[
            pl.BlockSpec(memory_space=pltpu.SMEM), row(width), row(width), full(gain), full(shift),
            full(w3), full(bias), full(rel_h), full(rel_w),
        ],
        out_specs=[
            row(width), row(width),
            pl.BlockSpec((2, PADW, 3 * local), lambda i: (i, 0, 0)),
            pl.BlockSpec((2, heads, PADW, PADW), lambda i: (i, 0, 0, 0)),
            row(local),
            pl.BlockSpec((1, width), lambda i: (0, 0)),
        ],
        out_shape=[
            jax.ShapeDtypeStruct((rows, width), BF16),
            jax.ShapeDtypeStruct((rows, width), BF16),
            jax.ShapeDtypeStruct((2 * steps, PADW, 3 * local), BF16),
            jax.ShapeDtypeStruct((2 * steps, heads, PADW, PADW), BF16),
            jax.ShapeDtypeStruct((rows, local), F32),
            jax.ShapeDtypeStruct((1, width), F32),
        ],
        scratch_shapes=[
            pltpu.VMEM((step, 3 * local), F32), pltpu.VMEM((128, 256), BF16), pltpu.VMEM((PADW, 128), BF16),
            pltpu.VMEM((PADW, 128), BF16), pltpu.VMEM((PADW, 128), jnp.int32),
        ],
        compiler_params=pltpu.CompilerParams(vmem_limit_bytes=48 << 20),
        cost_estimate=cost(25),
        name="attention_forward",
    )(first, tokens, cot, gain, shift, w3, bias, rel_h, rel_w)


def bwd_kernel(dctx_ref, qkv_ref, prob_ref, relh_ref, relw_ref, dqkv_ref, drel_ref, sum_ref, pad_ref, low_ref,
               rel_ref, once_ref, tab_ref):
    @pl.when(pl.program_id(0) == 0)
    def _():
        drel_ref[...] = jnp.zeros_like(drel_ref)
        sum_ref[...] = jnp.zeros_like(sum_ref)
        pad_ref[...] = jnp.zeros_like(pad_ref)
        rel = rel_tables(relh_ref[...], relw_ref[...], 0)
        rel_ref[:, :128], rel_ref[:, 128:] = rel, rel
        once_ref[...], tab_ref[...] = key_table(0.0), shift_table()

    width = dctx_ref.shape[1]
    low_half = half_lanes()
    once = once_ref[...]
    rel2 = rel_ref[...]
    scale = jnp.asarray(SCALE, BF16)
    for w in range(2):
        pad_ref[:TOK, :] = dctx_ref[w * TOK:(w + 1) * TOK, :]
        for p in range(width // 128):
            q = qkv_ref[w, :, p * 128:(p + 1) * 128]
            k = qkv_ref[w, :, width + p * 128:width + (p + 1) * 128] * scale
            v = qkv_ref[w, :, 2 * width + p * 128:2 * width + (p + 1) * 128]
            qs = q * scale
            do = pad_ref[:, p * 128:(p + 1) * 128].astype(BF16)
            zero = jnp.zeros_like(do)
            dv, dk, dqx = [], [], []
            for e in range(2):
                mine = low_half if e == 0 else ~low_half
                pr = prob_ref[w, 2 * p + e]
                dp = mm(v, jnp.where(mine, do, zero), NT)
                dv.append(mm(pr, do))
                p32 = pr.astype(F32)
                ds = (p32 * (dp - jnp.sum(dp * p32, axis=0, keepdims=True))).astype(BF16)
                dk.append(mm(ds, qs))
                dqx.append(mm(ds, jnp.where(mine, k, once), TN))
            near = jnp.where(low_half, dqx[1], dqx[0])
            tab = tab_ref[...]
            for b in range(4):
                near = jnp.where((tab & (1 << b)) != 0, pltpu.roll(near, 1 << b, 1), near)
            high = near.astype(BF16)
            rest = (near - high.astype(F32)).astype(BF16)
            both = jnp.concatenate([high, rest], 1)
            dq = jnp.where(low_half, dqx[0], dqx[1]) + mm(both, rel2, NT)
            drel_ref[...] += mm(q, both, TN)
            for t, g in enumerate((dq, jnp.where(low_half, dk[0], dk[1]), jnp.where(low_half, dv[0], dv[1]))):
                low_ref[t, w * TOK:(w + 1) * TOK, p * 128:(p + 1) * 128] = g[:TOK]
    for t in range(3):
        g = low_ref[t].astype(BF16)
        dqkv_ref[t] = g
        sum_ref[t:t + 1, :] += jnp.sum(g.astype(F32), axis=0, keepdims=True)


def bwd_more_kernel(dctx_ref, qkv_ref, prob_ref, relh_ref, relw_ref, _, *rest):
    bwd_kernel(dctx_ref, qkv_ref, prob_ref, relh_ref, relw_ref, *rest)


def attention_backward(dctx, qkv, prob, rel_h, rel_w, part, parts, done=None):
    rows, local = dctx.shape
    heads = local // HEAD_DIM
    step = 2 * TOK
    steps = rows // step // parts
    at = part * steps
    more = [] if done is None else [done]
    kernel = bwd_kernel if done is None else bwd_more_kernel
    return pl.pallas_call(
        kernel,
        grid=(steps,),
        input_output_aliases={} if done is None else {5: 0},
        in_specs=[
            pl.BlockSpec((step, local), lambda i: (i + at, 0)),
            pl.BlockSpec((2, PADW, 3 * local), lambda i: (i + at, 0, 0)),
            pl.BlockSpec((2, heads, PADW, PADW), lambda i: (i + at, 0, 0, 0)),
            full(rel_h), full(rel_w),
        ] + [pl.BlockSpec(memory_space=pl.ANY) for _ in more],
        out_specs=[
            pl.BlockSpec((3, step, local), lambda i: (0, i + at, 0)),
            pl.BlockSpec((128, 256), lambda i: (0, 0)),
            pl.BlockSpec((8, local), lambda i: (0, 0)),
        ],
        out_shape=[
            jax.ShapeDtypeStruct((3, rows, local), BF16),
            jax.ShapeDtypeStruct((128, 256), F32),
            jax.ShapeDtypeStruct((8, local), F32),
        ],
        scratch_shapes=[
            pltpu.VMEM((PADW, local), F32), pltpu.VMEM((3, step, local), F32), pltpu.VMEM((128, 256), BF16),
            pltpu.VMEM((PADW, 128), BF16), pltpu.VMEM((PADW, 128), jnp.int32),
        ],
        compiler_params=pltpu.CompilerParams(vmem_limit_bytes=48 << 20),
        cost_estimate=cost(13.5),
        name="attention_backward",
    )(dctx, qkv, prob, rel_h, rel_w, *more)


def split_rel(acc):
    acc = acc[:, :128] + acc[:, 128:]
    near = (acc[:64, 64:] + acc[64:, :64]).T
    return near[26::-1], near[58:31:-1]


def row_spec(n):
    return pl.BlockSpec((2 * TOK, n), lambda i: (i, 0))


def accumulate(ref, rows):
    @pl.when(pl.program_id(0) == 0)
    def _():
        ref[...] = jnp.zeros_like(ref)

    for i, r in enumerate(rows):
        ref[i:i + 1, :] += jnp.sum(r, axis=0, keepdims=True)


def mlp_half(h, low, w1, b1, w2, act_ref, pre_ref, sum_ref):
    u = mm(h, w1) + b1
    cdf = 0.5 * (1.0 + lax.erf(u * 0.7071067811865476))
    act_ref[...] = (u * cdf).astype(BF16)
    slope = cdf + u * jnp.exp(-0.5 * u * u) * 0.3989422804014327
    d = (mm(low, w2, NT) * slope).astype(BF16)
    pre_ref[...] = d
    accumulate(sum_ref, [d.astype(F32)])


def mlp_first_kernel(tok_ref, ctx_ref, oth_ref, low_ref, wp_ref, wpo_ref, pb_ref, gain_ref, shift_ref, w1_ref, b1_ref,
                     w2_ref, y_ref, hid_ref, act_ref, pre_ref, sum_ref, wpo16_ref):
    @pl.when(pl.program_id(0) == 0)
    def _():
        wpo16_ref[...] = wpo_ref[...].astype(BF16)

    proj = mm(ctx_ref[...].astype(BF16), wp_ref[...]) + mm(oth_ref[...].astype(BF16), wpo16_ref[...])
    y = tok_ref[...].astype(F32) + proj + pb_ref[...]
    y_ref[...] = y
    cen = y - jnp.mean(y, axis=1, keepdims=True)
    var = jnp.mean(cen * cen, axis=1, keepdims=True)
    h = (cen * lax.rsqrt(var + EPS) * gain_ref[...] + shift_ref[...]).astype(BF16)
    hid_ref[...] = h
    mlp_half(h, low_ref[...], w1_ref[...], b1_ref[...], w2_ref[...], act_ref, pre_ref, sum_ref)


def mlp_second_kernel(hid_ref, low_ref, w1_ref, b1_ref, w2_ref, act_ref, pre_ref, sum_ref):
    mlp_half(hid_ref[...], low_ref[...], w1_ref[...], b1_ref[...], w2_ref[...], act_ref, pre_ref, sum_ref)


def half_weight_specs(width, units, part):
    return [
        pl.BlockSpec((width, units), lambda i: (0, part)),
        pl.BlockSpec((1, units), lambda i: (0, part)),
        pl.BlockSpec((units, width), lambda i: (part, 0)),
    ]


def mlp_first(tokens, ctx, oth, low, wp, wpo, pb, gain, shift, w1, b1, w2):
    rows, width = tokens.shape
    local, units = ctx.shape[1], w1.shape[1] // 2
    return pl.pallas_call(
        mlp_first_kernel,
        grid=(rows // (2 * TOK),),
        in_specs=[row_spec(width), row_spec(local), row_spec(local), row_spec(width), full(wp), full(wpo), full(pb),
                  full(gain), full(shift)] + half_weight_specs(width, units, 0),
        out_specs=[row_spec(width), row_spec(width), row_spec(units), row_spec(units),
                   pl.BlockSpec((1, units), lambda i: (0, 0))],
        out_shape=[
            jax.ShapeDtypeStruct((rows, width), F32),
            jax.ShapeDtypeStruct((rows, width), BF16),
            jax.ShapeDtypeStruct((rows, units), BF16),
            jax.ShapeDtypeStruct((rows, units), BF16),
            jax.ShapeDtypeStruct((1, units), F32),
        ],
        scratch_shapes=[pltpu.VMEM(wpo.shape, BF16)],
        compiler_params=pltpu.CompilerParams(vmem_limit_bytes=48 << 20),
        cost_estimate=cost(15.5),
        name="mlp_first",
    )(tokens, ctx, oth, low, wp, wpo, pb, gain, shift, w1, b1, w2)


def mlp_second(hid, low, w1, b1, w2):
    rows, width = hid.shape
    units = w1.shape[1] // 2
    return pl.pallas_call(
        mlp_second_kernel,
        grid=(rows // (2 * TOK),),
        in_specs=[row_spec(width), row_spec(width)] + half_weight_specs(width, units, 1),
        out_specs=[row_spec(units), row_spec(units), pl.BlockSpec((1, units), lambda i: (0, 0))],
        out_shape=[
            jax.ShapeDtypeStruct((rows, units), BF16),
            jax.ShapeDtypeStruct((rows, units), BF16),
            jax.ShapeDtypeStruct((1, units), F32),
        ],
        compiler_params=pltpu.CompilerParams(vmem_limit_bytes=48 << 20),
        cost_estimate=cost(8),
        name="mlp_second",
    )(hid, low, w1, b1, w2)


def norm_back(d, hat, rstd, gain):
    dh = d * gain
    return rstd * (dh - jnp.mean(dh, axis=1, keepdims=True) - hat * jnp.mean(dh * hat, axis=1, keepdims=True))


def norm_parts(x):
    cen = x - jnp.mean(x, axis=1, keepdims=True)
    rstd = lax.rsqrt(jnp.mean(cen * cen, axis=1, keepdims=True) + EPS)
    return cen * rstd, rstd


def norm_two_kernel(part_ref, oth_ref, y_ref, low_ref, gain_ref, wp_ref, dy_ref, attn_ref, dctx_ref, sum_ref):
    d = part_ref[...] + oth_ref[...]
    hat, rstd = norm_parts(y_ref[...])
    dy = low_ref[...].astype(F32) + norm_back(d, hat, rstd, gain_ref[...])
    dy_ref[...] = dy
    low = dy.astype(BF16)
    attn_ref[...] = low
    dctx_ref[...] = mm(low, wp_ref[...], NT)
    accumulate(sum_ref, [d * hat, d, dy])


def norm_two_back(part, oth, y, low, gain, wp):
    rows, width = y.shape
    local = wp.shape[0]
    return pl.pallas_call(
        norm_two_kernel,
        grid=(rows // (2 * TOK),),
        in_specs=[row_spec(width)] * 4 + [full(gain), full(wp)],
        out_specs=[row_spec(width), row_spec(width), row_spec(local), pl.BlockSpec((8, width), lambda i: (0, 0))],
        out_shape=[
            jax.ShapeDtypeStruct((rows, width), F32),
            jax.ShapeDtypeStruct((rows, width), BF16),
            jax.ShapeDtypeStruct((rows, local), F32),
            jax.ShapeDtypeStruct((8, width), F32),
        ],
        compiler_params=pltpu.CompilerParams(vmem_limit_bytes=48 << 20),
        cost_estimate=cost(10),
        name="norm_two_back",
    )(part, oth, y, low, gain, wp)


def norm_one_kernel(first_ref, part_ref, oth_ref, tok_ref, dy_ref, gain_ref, dtok_ref):
    keep = keep_rows(first_ref[0] + 2 * pl.program_id(0))
    d = (part_ref[...] + oth_ref[...]) * keep
    hat, rstd = norm_parts(tok_ref[...].astype(F32))
    dtok_ref[...] = (dy_ref[...] + norm_back(d, hat, rstd, gain_ref[...].astype(F32))).astype(BF16)


def norm_one_back(first, part, oth, tokens, dy, gain):
    rows, width = tokens.shape
    return pl.pallas_call(
        norm_one_kernel,
        grid=(rows // (2 * TOK),),
        in_specs=[pl.BlockSpec(memory_space=pltpu.SMEM)] + [row_spec(width)] * 4 + [full(gain)],
        out_specs=row_spec(width),
        out_shape=jax.ShapeDtypeStruct((rows, width), BF16),
        compiler_params=pltpu.CompilerParams(vmem_limit_bytes=48 << 20),
        cost_estimate=cost(9),
        name="norm_one_back",
    )(first, part, oth, tokens, dy, gain)


def output_kernel(first_ref, part_ref, oth_ref, y_ref, bias_ref, out_ref):
    keep = keep_rows(first_ref[0] + 2 * pl.program_id(0))
    mlp = (part_ref[...] + oth_ref[...]) + bias_ref[...]
    out_ref[...] = (keep * (y_ref[...] + mlp)).astype(BF16)


def block_output(first, part, oth, y, bias):
    rows, width = y.shape
    return pl.pallas_call(
        output_kernel,
        grid=(rows // (2 * TOK),),
        in_specs=[pl.BlockSpec(memory_space=pltpu.SMEM)] + [row_spec(width)] * 3 + [full(bias)],
        out_specs=row_spec(width),
        out_shape=jax.ShapeDtypeStruct((rows, width), BF16),
        compiler_params=pltpu.CompilerParams(vmem_limit_bytes=48 << 20),
        cost_estimate=cost(7),
        name="block_output",
    )(first, part, oth, y, bias)


BIG = pltpu.CompilerParams(vmem_limit_bytes=48 << 20)


def grad_kernel(na, nb, *refs):
    a_refs, b_refs, out_ref = refs[:na], refs[na:na + nb], refs[-1]
    n = b_refs[0].shape[-1]

    def store(a_ref):
        a = a_ref[...]
        for k, b_ref in enumerate(b_refs):
            out_ref[:, k * n:(k + 1) * n] = mm(a, b_ref[...], TN)

    if na == 1:
        store(a_refs[0])
    else:
        half = pl.num_programs(0) // 2
        pl.when(pl.program_id(0) < half)(lambda: store(a_refs[0]))
        pl.when(pl.program_id(0) >= half)(lambda: store(a_refs[1]))


def weight_grad(a_list, b_list):
    rows, m = a_list[0].shape
    n = b_list[0].shape[1]
    tile = 256
    per = m // tile
    last = per - 1
    if len(a_list) == 1:
        a_specs = [pl.BlockSpec((rows, tile), lambda i: (0, i))]
    else:
        a_specs = [pl.BlockSpec((rows, tile), lambda i: (0, jnp.minimum(i, last))),
                   pl.BlockSpec((rows, tile), lambda i: (0, jnp.maximum(i - per, 0)))]
    return pl.pallas_call(
        functools.partial(grad_kernel, len(a_list), len(b_list)),
        grid=(per * len(a_list),),
        in_specs=a_specs + [full(b) for b in b_list],
        out_specs=pl.BlockSpec((tile, n * len(b_list)), lambda i: (i, 0)),
        out_shape=jax.ShapeDtypeStruct((m * len(a_list), n * len(b_list)), F32),
        compiler_params=BIG, cost_estimate=cost(6), name="weight_grad",
    )(*a_list, *b_list)


def rest_grad_kernel(hid_ref, d_ref, ctx_ref, attn_ref, out_ref):
    hid = hid_ref[...]
    for t in range(3):
        out_ref[t] = mm(hid, d_ref[t], TN)
    out_ref[3] = mm(ctx_ref[...].astype(BF16), attn_ref[...], TN)


def rest_grad(hid, dqkv, ctx, attn):
    rows, width = hid.shape
    local = dqkv.shape[2]
    tile = 128
    few = local // tile
    return pl.pallas_call(
        rest_grad_kernel,
        grid=(width // tile,),
        in_specs=[
            pl.BlockSpec((rows, tile), lambda i: (0, i)),
            full(dqkv),
            pl.BlockSpec((rows, tile), lambda i: (0, lax.rem(i, few))),
            pl.BlockSpec((rows, local), lambda i: (0, lax.div(i, few))),
        ],
        out_specs=pl.BlockSpec((4, tile, local), lambda i: (0, i, 0)),
        out_shape=jax.ShapeDtypeStruct((4, width, local), F32),
        compiler_params=BIG, cost_estimate=cost(8), name="rest_grad",
    )(hid, dqkv, ctx, attn)


def pair_kernel(dims, a0_ref, a1_ref, b0_ref, b1_ref, out_ref):
    out_ref[...] = mm(a0_ref[...], b0_ref[...], dims) + mm(a1_ref[...], b1_ref[...], dims)


def pair_product(a0, a1, b, dims):
    rows, k = a0.shape
    if dims is NN:
        n = b.shape[1]
        b_specs = [pl.BlockSpec((k, n), lambda i: (0, 0)), pl.BlockSpec((k, n), lambda i: (1, 0))]
    else:
        n = b.shape[0]
        b_specs = [pl.BlockSpec((n, k), lambda i: (0, 0)), pl.BlockSpec((n, k), lambda i: (0, 1))]
    return pl.pallas_call(
        functools.partial(pair_kernel, dims),
        grid=(rows // (2 * TOK),),
        in_specs=[row_spec(k), row_spec(k)] + b_specs,
        out_specs=row_spec(n),
        out_shape=jax.ShapeDtypeStruct((rows, n), F32),
        compiler_params=BIG, cost_estimate=cost(6.5), name="pair_product",
    )(a0, a1, b, b)


def triple_kernel(first_ref, d_ref, w_ref, tok_ref, out_ref, sum_ref):
    part = mm(d_ref[0], w_ref[0], NT) + mm(d_ref[1], w_ref[1], NT) + mm(d_ref[2], w_ref[2], NT)
    out_ref[...] = part
    masked = part * keep_rows(first_ref[0] + 2 * pl.program_id(0))
    hat, _ = norm_parts(tok_ref[...].astype(F32))
    accumulate(sum_ref, [masked * hat, masked])


def triple_product(first, d, w3, tokens):
    rows, local = d.shape[1:]
    n = w3.shape[1]
    return pl.pallas_call(
        triple_kernel,
        grid=(rows // (2 * TOK),),
        in_specs=[pl.BlockSpec(memory_space=pltpu.SMEM), pl.BlockSpec((3, 2 * TOK, local), lambda i: (0, i, 0)),
                  full(w3), row_spec(n)],
        out_specs=[row_spec(n), pl.BlockSpec((8, n), lambda i: (0, 0))],
        out_shape=[jax.ShapeDtypeStruct((rows, n), F32), jax.ShapeDtypeStruct((8, n), F32)],
        compiler_params=BIG, cost_estimate=cost(6), name="triple_product",
    )(first, d, w3, tokens)


def wait_for(arrays, token):
    return arrays if token is None else lax.optimization_barrier((arrays, token))[0]


def place_kernel(counts, at_ref, *refs):
    out_ref, step, at = refs[-1], pl.program_id(0), 0
    for piece, n in zip(refs, counts):
        @pl.when((step >= at) & (step < at + n))
        def _(piece=piece):
            out_ref[...] = piece[...]
        at += n


def place(pieces, starts, rows):
    cols = pieces[0].shape[1]
    tile = tiles_of(min(a.shape[0] for a in pieces), cols)
    counts = [a.shape[0] // tile for a in pieces]
    firsts = [sum(counts[:i]) for i in range(len(counts))]
    spots = jnp.stack([jnp.asarray(s, jnp.int32) // tile + j for s, n in zip(starts, counts) for j in range(n)])
    maps = [lambda i, at, f=f, n=n: jnp.clip(i - f, 0, n - 1) for f, n in zip(firsts, counts)]
    out = jax.ShapeDtypeStruct((rows, cols), F32)
    return blocks_call(functools.partial(place_kernel, counts), spots, (sum(counts),), pieces, maps, tile,
                       [lambda i, at: at[i]], [out], "place")[0]


def cut_kernel(at_ref, a_ref, b_ref, out_a_ref, out_b_ref):
    out_a_ref[...], out_b_ref[...] = a_ref[...], b_ref[...]


def cut(g, starts, rows):
    tile = tiles_of(rows, g.shape[1])
    one = jax.ShapeDtypeStruct((rows, g.shape[1]), F32)
    return blocks_call(cut_kernel, jnp.stack([s // tile for s in starts]), (rows // tile,), [g, g],
                       [lambda i, at, k=k: at[k] + i for k in range(2)], tile, [lambda i, at: i] * 2, [one, one], "cut")


def blocks_call(body, scalars, grid, arrays, in_maps, tile, out_maps, outs, name):
    spec = lambda a, f: pl.BlockSpec((tile, a.shape[1]), lambda *i, f=f: (f(*i), 0))
    return pl.pallas_call(
        body,
        grid_spec=pltpu.PrefetchScalarGridSpec(
            num_scalar_prefetch=1, grid=grid,
            in_specs=[spec(a, f) for a, f in zip(arrays, in_maps)],
            out_specs=[spec(o, f) for o, f in zip(outs, out_maps)],
        ),
        out_shape=outs, compiler_params=BIG, cost_estimate=step_cost(), name=name,
    )(scalars, *arrays)


def spread_kernel(at_ref, x_ref, y_ref, d0_ref, d1_ref, to_x_ref, to_y_ref):
    half = pl.program_id(0)
    x, y = x_ref[...], y_ref[...]
    to_x_ref[...] = jnp.where(half == 1, x + d1_ref[...], x)
    to_y_ref[...] = jnp.where(half == 0, y + d0_ref[...], y)


def sum_split_kernel(count, at_ref, *refs):
    out = keep = 0.0
    for a in refs[:count]:
        out = out + a[...]
    for a in refs[count:2 * count]:
        keep = keep + a[...]
    refs[-2][...], refs[-1][...] = out, keep


def tiles_of(rows, cols):
    return max(t for t in range(8, rows + 1, 8) if rows % t == 0 and t * cols <= 150000)


def sum_split(arrays, bases, bit, rows, name):
    cols = arrays[0].shape[1]
    tile = tiles_of(rows, cols)
    per = rows // tile
    scalars = jnp.stack([jnp.asarray(b, jnp.int32) // tile for b in bases] + [(1 - bit) * per, bit * per])
    n = len(arrays)
    maps = [lambda i, at, k=k, h=h: at[k] + at[n + h] + i for h in range(2) for k in range(n)]
    one = jax.ShapeDtypeStruct((rows, cols), F32)
    return blocks_call(functools.partial(sum_split_kernel, n), scalars, (per,), list(arrays) * 2, maps, tile,
                       [lambda i, at: i] * 2, [one, one], name)


class Plane:
    def __init__(self, g, bits):
        self.x, self.y, self.b0, self.b1 = bits
        self.rows, self.cols = g.shape
        self.h = self.rows // 8
        self.live = (g,)

    def step(self, name, token):
        self.live, token = getattr(self, name)(*wait_for(self.live, token))
        return token

    def send(self, a, stride):
        n = lax.axis_size("dp")
        return lax.ppermute(a, "dp", [(i, i ^ stride) for i in range(n)])

    def slab(self, x, y):
        return (2 * x + y) * 2 * self.h

    def s1(self, g):
        far = self.slab(1 - self.x, 1 - self.y)
        d0, d1 = cut(g, (far, far + self.h), self.h)
        return (g, self.send(d0, 1), self.send(d1, 2)), d0

    def s2(self, g, d0, d1):
        x, y, h = self.x, self.y, self.h
        tile = tiles_of(h, self.cols)
        per = h // tile
        scalars = jnp.stack([self.slab(1 - x, y) // tile, self.slab(x, 1 - y) // tile])
        one = jax.ShapeDtypeStruct((2 * h, self.cols), F32)
        to_x, to_y = blocks_call(
            spread_kernel, scalars, (2, per), [g, g, d0, d1],
            [lambda k, i, at: at[0] + k * per + i, lambda k, i, at: at[1] + k * per + i,
             lambda k, i, at: i, lambda k, i, at: i],
            tile, [lambda k, i, at: k * per + i] * 2, [one, one], "spread")
        return (g, self.send(to_x, 1), self.send(to_y, 2)), to_x

    def z1(self, g, rx, ry):
        out, keep = sum_split((g, rx, ry), (self.slab(self.x, self.y), 0, 0), self.b0, self.h, "sum_xy")
        return (keep, self.send(out, 4)), out

    def z2(self, keep, r):
        out, keep = sum_split((keep, r), (0, 0), self.b1, keep.shape[0] // 2, "sum_near")
        return (keep, self.send(out, 8)), out

    def z3(self, keep, r):
        c = lax.optimization_barrier(keep + r)
        return (c, self.send(c, 8)), c

    def z4(self, c, o):
        n = c.shape[0]
        h = place((c, o), (self.b1 * n, (1 - self.b1) * n), 2 * n)
        return (h, self.send(h, 4)), h

    def g1(self, h, o):
        n = h.shape[0]
        w = place((h, o), (self.b0 * n, (1 - self.b0) * n), 2 * n)
        return (w, self.send(w, 1), self.send(w, 2)), w

    def g2(self, w, rx, ry):
        n = w.shape[0] // 2
        a, b = lax.optimization_barrier((ry[:n], rx[n:]))
        return (w, rx, ry, self.send(a, 1), self.send(b, 2)), a

    def end(self, w, rx, ry, d0, d1):
        x, y, h = self.x, self.y, self.h
        far = self.slab(1 - x, 1 - y)
        self.total = place((w, rx, ry, d0, d1), (self.slab(x, y), self.slab(1 - x, y), self.slab(x, 1 - y), far, far + h),
                           self.rows)
        return (), self.total


class Butterfly(Plane):
    def t1(self, g):
        return (g, self.send(g, 1)), g

    def turn(self, stride, g, r):
        g = lax.optimization_barrier(g + r)
        return (g, self.send(g, stride)), g

    def t2(self, g, r):
        return self.turn(2, g, r)

    def t3(self, g, r):
        return self.turn(4, g, r)

    def t4(self, g, r):
        return self.turn(8, g, r)

    def end(self, g, r):
        self.total = lax.optimization_barrier(g + r)
        return (), self.total


def swap(a):
    return lax.ppermute(a, "tensor", [(0, 1), (1, 0)])


class Block:
    def __init__(self, args):
        (self.tokens, self.cot, w_qkv, qv_bias, self.w_proj, proj_bias, self.w_fc1, fc1_bias, self.w_fc2, fc2_bias,
         gain_one, shift_one, gain_two, shift_two, rel_h, rel_w) = args
        self.rows, self.width = self.tokens.shape
        self.local = w_qkv.shape[2]
        self.units = self.w_fc1.shape[1] // 2
        self.rel_shape = rel_h.shape
        index = lax.axis_index("dp")
        self.first = jnp.reshape(index * (self.rows // TOK), (1,)).astype(jnp.int32)
        self.bits = tuple((index >> b) & 1 for b in range(4))
        line = lambda v: v.astype(F32)[None]
        self.g1, self.s1, self.g2, self.s2 = gain_one[None], shift_one[None], line(gain_two), line(shift_two)
        self.pb, self.b1, self.b2 = line(proj_bias), line(fc1_bias), line(fc2_bias)
        self.w3 = jnp.transpose(w_qkv, (1, 0, 2))
        self.qv_bias = qv_bias
        self.rel_h, self.rel_w = rel_h, rel_w
        self.grads = {}

    def K1(self, token):
        other = swap(self.w_proj.astype(F32))
        self.hid1, self.low, self.qkv, self.prob, self.ctx, self.d_fc2_bias = attention_forward(
            self.first, self.tokens, self.cot, self.g1, self.s1, self.w3, self.qv_bias, self.rel_h, self.rel_w)
        self.ctx_other, self.proj_other = swap(self.ctx), other
        return self.ctx

    def K2a(self, token):
        ctx = wait_for(self.ctx, token)
        self.y, self.hid2, self.act0, self.pre0, self.sum0 = mlp_first(
            self.tokens, ctx, self.ctx_other, self.low, self.w_proj, self.proj_other, self.pb, self.g2, self.s2,
            self.w_fc1, self.b1, self.w_fc2)
        return self.hid2

    def K2b(self, token):
        hid = wait_for(self.hid2, token)
        self.act1, self.pre1, self.sum1 = mlp_second(hid, self.low, self.w_fc1, self.b1, self.w_fc2)
        return self.act1

    def grad(self, name, a_list, b_list, token):
        a_list = wait_for(a_list, token)
        self.grads[name] = weight_grad(a_list, b_list)
        return self.grads[name]

    def dw2a(self, token):
        return self.grad("A0", [self.act0], [self.low], token)

    def dw2b(self, token):
        return self.grad("A1", [self.act1], [self.low], token)

    def dw2(self, token):
        return self.grad("A", [self.act0, self.act1], [self.low], token)

    def dw1a(self, token):
        return self.grad("B0", [self.hid2], [self.pre0], token)

    def dw1b(self, token):
        return self.grad("B1", [self.hid2], [self.pre1], token)

    def dw1(self, token):
        return self.grad("B", [self.hid2], [self.pre0, self.pre1], token)

    def dh2(self, token):
        pre = wait_for(self.pre0, token)
        self.dh2_part = pair_product(pre, self.pre1, self.w_fc1, NT)
        return self.dh2_part

    def fc2(self, token):
        act = wait_for(self.act0, token)
        self.fc2_part = pair_product(act, self.act1, self.w_fc2, NN)
        return self.fc2_part

    def xd(self, token):
        part = wait_for(self.dh2_part, token)
        self.dh2_other = swap(part)
        return part

    def xf(self, token):
        part = wait_for(self.fc2_part, token)
        self.fc2_other = swap(part)
        return part

    def xh(self, token):
        part = wait_for(self.dh1_part, token)
        self.dh1_other = swap(part)
        return part

    def K3(self, token):
        y = wait_for(self.y, token)
        self.dy, self.d_attn, self.dctx, self.sum_two = norm_two_back(
            self.dh2_part, self.dh2_other, y, self.low, self.g2, self.w_proj)
        return self.dctx

    def K4a(self, token):
        dctx = wait_for(self.dctx, token)
        self.dqkv, self.acc0, self.bias0 = attention_backward(
            dctx, self.qkv, self.prob, self.rel_h, self.rel_w, 0, 2)
        return self.acc0

    def K4b(self, token):
        dctx = wait_for(self.dctx, token)
        self.dqkv, self.acc1, self.bias1 = attention_backward(
            dctx, self.qkv, self.prob, self.rel_h, self.rel_w, 1, 2, self.dqkv)
        return self.acc1

    def dh1(self, token):
        d = wait_for(self.dqkv, token)
        self.dh1_part, self.sum_one = triple_product(self.first, d, self.w3, self.tokens)
        return self.dh1_part

    def dwr(self, token):
        hid = wait_for(self.hid1, token)
        self.grads["C"] = rest_grad(hid, self.dqkv, self.ctx, self.d_attn).reshape(4 * self.width, self.local)
        return self.grads["C"]

    def vec(self, token):
        bias_qv = self.bias0 + self.bias1
        rel_h, rel_w = split_rel(self.acc0 + self.acc1)
        shared = jnp.concatenate([self.sum_one[:2].reshape(-1), rel_h.reshape(-1), rel_w.reshape(-1)])
        lines = [shared, self.sum_two[:3].reshape(-1), self.d_fc2_bias[0], self.sum0[0], self.sum1[0],
                 bias_qv[0], bias_qv[2]]
        self.small_sizes = [a.shape[0] for a in lines]
        flat = jnp.concatenate(lines)
        flat = wait_for(jnp.pad(flat, (0, -flat.shape[0] % (8 * self.width))).reshape(-1, self.width), token)
        self.grads["S"] = flat
        return flat

    def K5(self, token):
        dy = wait_for(self.dy, token)
        self.d_tokens = norm_one_back(
            self.first, self.dh1_part, self.dh1_other, self.tokens, dy, self.g1)
        return self.d_tokens

    def K6(self, token):
        y = wait_for(self.y, token)
        self.output = block_output(self.first, self.fc2_part, self.fc2_other, y, self.b2)
        return self.output

    def results(self, total):
        n, w, rel = self.local, self.width, self.rel_shape
        sums = total["C"]
        dw_qkv = jnp.transpose(sums[:3 * w].reshape(3, w, n), (1, 0, 2))
        halves = sums[3 * w:].reshape(w // n, n, n)
        dw_proj = jnp.concatenate([halves[i] for i in range(w // n)], 1)
        flat, cuts, at = total["S"].reshape(-1), [], 0
        for size in self.small_sizes:
            cuts.append(flat[at:at + size])
            at += size
        cuts[0] = cuts[0] + swap(cuts[0])
        shared, two, fc2b, b1a, b1b, qb, vb = cuts
        count = rel[0] * rel[1]
        tables = shared[2 * w:]
        return (self.output, self.d_tokens, dw_qkv, jnp.stack([qb, vb]), dw_proj, two[2 * w:], total["B"],
                jnp.concatenate([b1a, b1b]), total["A"], fc2b, shared[:w], shared[w:2 * w], two[:w], two[w:2 * w],
                tables[:count].reshape(rel), tables[count:2 * count].reshape(rel))


ORDER = (
    "K1", "K2a", "K2b", "dh2", "xd", "dw2", "A.s1", "K3", "A.s2", "dw1", "K4a", "A.z1", "B.s1", "K4b", "A.z2", "B.s2", "dh1", "A.z3", "dwr", "B.z1", "C.s1", "xh", "fc2", "A.z4",
    "B.z2", "C.s2", "xf", "K5", "K6", "A.g1", "B.z3", "C.z1", "A.g2", "B.z4", "C.z2", "vec", "S.t1", "A.end", "B.g1", "C.z3", "S.t2", "B.g2", "C.z4", "S.t3", "B.end",
    "C.g1", "S.t4", "C.g2", "S.end", "C.end",
)


def shards(*args):
    block = Block(args)
    token, sums, ordered = None, {}, lax.axis_size("dp") == 16
    for item in ORDER:
        if "." not in item:
            token = getattr(block, item)(token)
        elif ordered:
            name, step = item.split(".")
            if name not in sums:
                sums[name] = (Butterfly if name == "S" else Plane)(block.grads[name], block.bits)
            token = sums[name].step(step, token)
    if ordered:
        total = {name: s.total for name, s in sums.items()}
    else:
        total = lax.psum(block.grads, "dp")
    return block.results(total)


def solution(mesh):
    rows, rep = P("dp", None), P()
    ins = (rows, rows, P(None, None, "tensor"), P(None, "tensor"), P("tensor", None), rep, P(None, "tensor"),
           P("tensor"), P("tensor", None), rep, rep, rep, rep, rep, rep, rep)
    return jax.shard_map(shards, mesh=mesh, in_specs=ins, out_specs=ins, check_vma=False)
```
